512 devices in a mesh: ep: 64 (over y_lo, z, core), dp: 8 (over y_hi, x).
Axes of the slice: x: 4, y: 4 (y_hi: 2, y_lo: 2; y = y_hi * 2 + y_lo), z: 16, core: 2. Of those that a mesh axis runs over, the one named last changes fastest.
Arguments:
- out_grad: bfloat16 [65536, 3584], P(('ep', 'dp')), may hold values from -6 to 6
- expert_ids: int32 [65536, 2], P(('ep', 'dp')), may hold values from 0 to 63, all different within a row; in each aligned block of 128 rows (0 to 127, 128 to 255, ...) at most 6 rows name the same one
- combine: float32 [65536, 2], P(('ep', 'dp')), may hold values from 0.1 to 1
- router_logits: bfloat16 [65536, 384], P(('ep', 'dp')), may hold values from -16 to 250
- saved_hidden: bfloat16 [64, 3072, 1024], P('ep', 'dp'), may hold values from -6 to 6
- weight: bfloat16 [64, 1024, 3584], P('ep', 'dp'), may hold values from -0.1875 to 0.1875
- moment_one: bfloat16 [64, 1024, 3584], P('ep', 'dp'), may hold values from -6 to 6
- moment_two: bfloat16 [64, 1024, 3584], P('ep', 'dp'), may hold values from 2 to 40
- next_hidden: bfloat16 [64, 256, 1024], P('ep', 'dp'), may hold values from -6 to 6
Outputs:
- refreshed: bfloat16 [64, 256, 3584], P('ep', 'dp')
- router_grad: bfloat16 [65536, 384], P(('ep', 'dp'))
The draws below stay inside these ranges and needn't reach their ends.
Inputs may be any that keep to these rules, and one draw needn't show every extreme that they name: `expert_ids`: each row names 2 different experts; among the 128 rows of one device no expert is named more than 6 times, a bound that some block reaches.
All inputs are finite; a program needn't handle non-finite values.
Results may differ from the reference program's by a relative error of at most 0.014.
Values may be sent and summed in bfloat16 or wider, within the bound.
No kernel may reach another device: no remote copies, remote signals or barrier semaphores. Data moves between devices by JAX's collectives and lax.ppermute only.
A program may use at most 64 MiB of HBM per device.

```python
import math
import jax
import jax.numpy as jnp
import numpy as np
from jax import lax

D = 3584
FF = 1024
ROUTER = 384
TOPW = 2
TOK_DEV = 128
NEXT = 32
EXPERTS = 64
CAP = 6
TOKENS = 65536
N_EP = 64
N_DP = 8


def draw_router_logits(key, part):
    base_key = jax.random.fold_in(key, 0)
    return (3.0 * jax.random.truncated_normal(base_key, -5.0, 5.0, (TOKENS, ROUTER), jnp.float32)).astype(jnp.bfloat16)


def block_levels(key, dims, pieces, least, largest):
    def one(dim, parts):
        steps = jax.random.uniform(jax.random.fold_in(jax.random.fold_in(key, 6), dim), (parts,), jnp.float32, least / len(pieces), largest / len(pieces))
        return jnp.repeat(jnp.exp(steps), dims[dim] // parts).reshape((-1,) + (1,) * (len(dims) - dim - 1))

    factor_of = one(*pieces[0])
    for cut in pieces[1:]:
        factor_of = factor_of * one(*cut)
    return factor_of


def assign_block(key, own, number, rows, count, top, most, slope):
    sequence = jax.random.permutation(key, count)
    heavy_load, common = portions_of(count, rows * top, most, slope, True), portions_of(count, rows * top, most, slope, False)
    places = jnp.arange(count)

    def named(lengths, offset_by):
        used = int((lengths > 0).sum())
        fixed = max(1, used // 4)
        shifted = fixed + (places - fixed + offset_by * (used - fixed)) % max(1, count - fixed)
        return jnp.zeros((count,), jnp.int32).at[sequence[jnp.where(places < fixed, places, shifted)]].set(jnp.asarray(lengths, jnp.int32))

    lengths = jnp.where(number % 4 == 0, named(heavy_load, number // 4), named(common, number - number // 4 - 1))
    mixed = jax.random.permutation(jax.random.fold_in(own, 3), count)
    source_of, receiver = mixed[0:count // 2 * 2:2], mixed[1:count // 2 * 2:2]
    room = jnp.minimum(lengths[source_of] - 1, most - lengths[receiver]) // 2
    room = jnp.where((source_of == sequence[0]) | (receiver == sequence[0]) | (lengths[receiver] == 0), 0, jnp.maximum(room, 0))
    shifted = jax.random.randint(jax.random.fold_in(own, 4), (count // 2,), 0, 1 << 20) % (room + 1)
    lengths = lengths.at[source_of].add(-shifted).at[receiver].add(shifted)
    members = jnp.searchsorted(jnp.cumsum(lengths), jnp.arange(rows * top), side="right").astype(jnp.int32)
    table = members.reshape(top, rows).T
    table = table[jax.random.permutation(jax.random.fold_in(own, 1), rows)]
    offset_by = jax.random.randint(jax.random.fold_in(own, 2), (rows, 1), 0, top)
    return jnp.take_along_axis(table, (jnp.arange(top)[None, :] + offset_by) % top, axis=1)


def portions_of(amount, total, limit, slope, full):
    portions = [(1 << 20) // math.isqrt(rank ** slope) + 1 for rank in range(1, amount + 1)]
    largest = limit if full else min(limit, max(-(-total // amount), total * portions[0] // sum(portions)))
    least = 1 if total - largest >= amount - 1 else 0
    holding, spare = [largest] + [least] * (amount - 1), total - largest - least * (amount - 1)
    while spare > 0:
        movable = [i for i in range(1, amount) if holding[i] < largest] or [i for i in range(1, amount) if holding[i] < limit]
        pool, left = sum([portions[i] for i in movable]), spare
        for i in movable:
            addition = min(limit - holding[i], max(1, left * portions[i] // pool), spare)
            holding[i] = holding[i] + addition
            spare = spare - addition
    return np.array(holding)


def noise(rng, extent, scale, bound, shards=(), kind=jnp.bfloat16):
    values = scale * jax.random.normal(rng, extent, jnp.float32)
    if shards:
        values = values * block_levels(rng, extent, shards, -0.22, 0.18)
    return jnp.clip(values, -bound, bound).astype(kind)


def setup_inputs(seed: int = 0) -> dict:
    key_list = jax.random.split(jax.random.key(seed), 10)
    out_grad = noise(key_list[0], (TOKENS, D), 1.0, 6.0, ((0, 512),))
    expert_ids_keys = jax.random.split(jax.random.fold_in(key_list[1], 1), TOKENS // TOK_DEV)
    expert_ids_turns = jax.random.permutation(jax.random.fold_in(key_list[1], 3), TOKENS // TOK_DEV)
    expert_ids = jax.vmap(lambda own, number: assign_block(jax.random.fold_in(key_list[1], 2), own, number, TOK_DEV, EXPERTS, TOPW, CAP, 2))(expert_ids_keys, expert_ids_turns).reshape((TOKENS, TOPW))
    combine = jnp.clip(0.1 + 0.9 * jax.random.uniform(key_list[2], (TOKENS, TOPW), jnp.float32) ** block_levels(key_list[2], (TOKENS, TOPW), ((0, 512),), -0.2, 0.2), 0.1, 1.0)
    router_logits = draw_router_logits(jax.random.fold_in(key_list[9], 71), 0)
    saved_hidden = noise(key_list[4], (EXPERTS, N_DP * N_EP * CAP, FF), 1.0, 6.0, ((0, 64), (1, 8)))
    weight = noise(key_list[5], (EXPERTS, FF, D), FF ** -0.5, 0.1875, ((0, 64), (1, 8)))
    moment_one = noise(key_list[6], (EXPERTS, FF, D), 1.0, 6.0, ((0, 64), (1, 8)))
    moment_two = jnp.clip(jnp.exp(math.log(40.0) - 2.9957323 * jax.random.uniform(key_list[7], (EXPERTS, FF, D), jnp.float32) ** block_levels(key_list[7], (EXPERTS, FF, D), ((0, 64), (1, 8)), -0.2, 0.2)), 2.0, 40.0).astype(jnp.bfloat16)
    next_hidden = noise(key_list[8], (EXPERTS, N_DP * NEXT, FF), 1.0, 6.0, ((0, 64), (1, 8)))
    return dict(out_grad=out_grad, expert_ids=expert_ids, combine=combine, router_logits=router_logits, saved_hidden=saved_hidden, weight=weight, moment_one=moment_one, moment_two=moment_two, next_hidden=next_hidden)


beta_one = 0.9
beta_two = 0.95
learn_rate = 0.2
decay_rate = 0.1
step_count = 100.0
adam_eps = 1e-08
zloss_coef = 0.25

def adamw(weight, first, second, gradient):
    first_new = beta_one * first.astype(jnp.float32) + (1.0 - beta_one) * gradient
    second_new = beta_two * second.astype(jnp.float32) + (1.0 - beta_two) * gradient * gradient
    first_hat = first_new / (1.0 - beta_one ** step_count)
    second_hat = second_new / (1.0 - beta_two ** step_count)
    current = weight.astype(jnp.float32)
    change = first_hat / (jnp.sqrt(second_hat) + adam_eps) + decay_rate * current
    return (current - learn_rate * change).astype(jnp.bfloat16)

def zloss_grad(logits):
    values = logits.astype(jnp.float32)
    row_max = lax.optimization_barrier(jnp.max(values, axis=-1, keepdims=True))
    log_total = row_max + jnp.log(lax.optimization_barrier(jnp.sum(jnp.exp(values - row_max), axis=-1, keepdims=True)))
    probs = jnp.exp(values - log_total)
    return (zloss_coef * 2.0 * log_total * probs).astype(jnp.bfloat16)

def reference(out_grad, expert_ids, combine, router_logits, saved_hidden, weight, moment_one, moment_two, next_hidden):
    blocks = TOKENS // TOK_DEV
    per_block = TOK_DEV * TOPW
    ids_block = expert_ids.reshape(blocks, per_block)
    onehot = (ids_block[:, :, None] == jnp.arange(EXPERTS, dtype=jnp.int32)[None, None, :]).astype(jnp.int32)
    before = jnp.cumsum(onehot, axis=1) - onehot
    slot_index = lax.optimization_barrier(jnp.sum(before * onehot, axis=2))
    block_index = jnp.arange(blocks, dtype=jnp.int32)[:, None]
    source = block_index // N_DP
    replica = block_index % N_DP
    row_index = replica * (N_EP * CAP) + source * CAP + slot_index
    total_pos = TOKENS * TOPW
    positions = jnp.arange(total_pos, dtype=jnp.int32)
    table = jnp.full((EXPERTS, N_DP * N_EP * CAP), total_pos, dtype=jnp.int32)
    table = table.at[expert_ids.reshape(-1), row_index.reshape(-1)].set(positions)

    def per_expert(expert):
        position = table[expert]
        valid = position < total_pos
        safe = jnp.minimum(position, total_pos - 1)
        token_index = safe // TOPW
        pick_index = safe % TOPW
        rows = out_grad[token_index].astype(jnp.float32)
        factor = combine[token_index, pick_index]
        sent = jnp.where(valid[:, None], factor[:, None] * rows, 0.0).astype(jnp.bfloat16)
        hidden = saved_hidden[expert].astype(jnp.float32).reshape(N_DP, N_EP * CAP, FF)
        sent_rows = sent.astype(jnp.float32).reshape(N_DP, N_EP * CAP, D)
        partial_value = jnp.einsum('jrf,jrd->jfd', hidden, sent_rows)
        rounded = lax.optimization_barrier(partial_value.astype(jnp.bfloat16))
        gradient = lax.optimization_barrier(jnp.sum(rounded.astype(jnp.float32), axis=0))
        updated = adamw(weight[expert], moment_one[expert], moment_two[expert], gradient)
        return jnp.dot(next_hidden[expert], updated, preferred_element_type=jnp.float32).astype(jnp.bfloat16)
    refreshed = lax.map(per_expert, jnp.arange(EXPERTS, dtype=jnp.int32))
    return (refreshed, zloss_grad(router_logits))
```

```python
import jax
import jax.numpy as jnp
from jax import lax
from jax.experimental import pallas as pl
from jax.experimental.pallas import tpu as pltpu
from jax.sharding import PartitionSpec as P

beta_one = 0.9
beta_two = 0.95
learn_rate = 0.2
decay_rate = 0.1
step_count = 100.0
adam_eps = 1e-08
zloss_coef = 0.25

LANE = 128
HALF = 64
META = 8
WIDE = 3
SPAN = WIDE * LANE


def adamw(weight, first, second, gradient):
    first_new = beta_one * first.astype(jnp.float32) + (1.0 - beta_one) * gradient
    second_new = beta_two * second.astype(jnp.float32) + (1.0 - beta_two) * gradient * gradient
    first_hat = first_new / (1.0 - beta_one**step_count)
    second_hat = second_new / (1.0 - beta_two**step_count)
    current = weight.astype(jnp.float32)
    change = first_hat / (jnp.sqrt(second_hat) + adam_eps) + decay_rate * current
    return (current - learn_rate * change).astype(jnp.bfloat16)


def zloss_grad(logits):
    values = logits.astype(jnp.float32)
    row_max = jnp.max(values, axis=-1, keepdims=True)
    log_total = row_max + jnp.log(jnp.sum(jnp.exp(values - row_max), axis=-1, keepdims=True))
    probs = jnp.exp(values - log_total)
    return (zloss_coef * 2.0 * log_total * probs).astype(jnp.bfloat16)


def iota(shape, dim):
    return lax.broadcasted_iota(jnp.int32, shape, dim)


def digits(value, *bases):
    found = []
    for base in reversed(bases):
        above = jnp.floor((value.astype(jnp.float32) + 0.5) * (1.0 / base)).astype(jnp.int32)
        found.append(value - above * base)
        value = above
    return found[::-1]


def slots_of(ids):
    tokens = ids[0].shape[1]
    wide = [jnp.broadcast_to(row, (tokens, tokens)) for row in ids]
    tall = [jnp.transpose(mat) for mat in wide]
    earlier = iota((tokens, tokens), 0) < iota((tokens, tokens), 1)
    counts = []
    for mat in wide:
        hits = jnp.where(earlier & (tall[0] == mat), 1.0, 0.0)
        hits = hits + jnp.where(earlier & (tall[1] == mat), 1.0, 0.0)
        counts.append(jnp.sum(hits, axis=0, keepdims=True))
    return counts


def own_block(replicas):
    def body(own_ref, ids_ref, combine_ref, grad_ref, *message_refs):
        ids = ids_ref[...].astype(jnp.float32)
        combine = combine_ref[...]
        tokens = ids.shape[1]
        pieces = [ids[0:1], ids[1:2]]
        for k in range(2):
            rest = combine[k : k + 1]
            for _ in range(3):
                part = rest.astype(jnp.bfloat16).astype(jnp.float32)
                pieces.append(part)
                rest = rest - part
        meta = jnp.concatenate(pieces, axis=0).astype(jnp.bfloat16)
        meta = jnp.concatenate([meta] * WIDE, axis=1)
        for r in range(replicas):
            start = pl.multiple_of((own_ref[0] ^ r) * SPAN, LANE)
            message_refs[r][0:tokens, :] = grad_ref[:, pl.ds(start, SPAN)]
            message_refs[r][tokens : tokens + META, :] = meta

    return body


def own_tail(experts, capacity, replicas):
    tiles = replicas * HALF // LANE
    half = capacity // 2
    rows = half * replicas

    def body(ids_ref, combine_ref, grad_ref, tail_ref):
        ids = ids_ref[...].astype(jnp.float32)
        combine = combine_ref[...]
        tokens = ids.shape[1]
        id_rows = [ids[0:1], ids[1:2]]
        slots = slots_of(id_rows)
        target = [
            (id_rows[k] * capacity + slots[k]).astype(jnp.int32)[:, None, :] for k in range(2)
        ]
        shape = (experts, rows, tokens)
        place = iota(shape, 1)
        group = jnp.zeros(shape, jnp.int32)
        for c in range(1, half):
            group = group + jnp.where(place >= c * replicas, 1, 0)
        owner = (place - group * replicas)[:, :, 0:LANE]
        outs = []
        for side in range(2):
            key = iota(shape, 0) * capacity + group + side * half
            spread = jnp.where(key == target[0], combine[0:1][:, None, :], 0.0) + jnp.where(
                key == target[1], combine[1:2][:, None, :], 0.0
            )
            scale = jnp.sum(spread, axis=2, keepdims=True)
            chosen = jnp.where(spread > 0.0, 1.0, 0.0).reshape(experts * rows, tokens)
            picked = jnp.dot(
                chosen.astype(jnp.bfloat16), grad_ref[...], preferred_element_type=jnp.float32
            ).reshape(experts, rows, tiles * LANE)
            out = picked[:, :, 0:LANE]
            for t in range(1, tiles):
                out = jnp.where(owner >= 2 * t, picked[:, :, t * LANE : (t + 1) * LANE], out)
            outs.append((out * scale).reshape(experts * rows, LANE))
        odd = (owner & 1).reshape(experts * rows, LANE) == 1
        left = iota((experts * rows, LANE), 1) < HALF
        low = jnp.where(odd, pltpu.roll(outs[0], HALF, 1), outs[0])
        high = jnp.where(odd, outs[1], pltpu.roll(outs[1], HALF, 1))
        tail_ref[...] = jnp.where(left, low, high).astype(jnp.bfloat16)

    return body


def own_columns(experts, capacity, replicas, tokens, group):
    def body(*refs):
        message_refs, (send_ref, tokens_ref, target_ref, weight_ref) = (
            refs[:replicas],
            refs[replicas:],
        )
        for r in range(replicas):
            tokens_ref[r * tokens : (r + 1) * tokens, :] = message_refs[r][0:tokens, :]
            meta = message_refs[r][tokens : tokens + META, 0:tokens].astype(jnp.float32)
            id_rows = [meta[0:1], meta[1:2]]
            slots = slots_of(id_rows)
            for k in range(2):
                where = id_rows[k] * (replicas * capacity) + slots[k] + float(r * capacity)
                target_ref[k : k + 1, r * tokens : (r + 1) * tokens] = where.astype(jnp.int32)
                first = 2 + 3 * k
                weight_ref[k : k + 1, r * tokens : (r + 1) * tokens] = (
                    meta[first : first + 1] + meta[first + 1 : first + 2]
                ) + meta[first + 2 : first + 3]
        height = replicas * capacity
        rows = group * height

        def step(i, carry):
            key = iota((rows, replicas * tokens), 0) + i * rows
            spread = jnp.where(
                key == target_ref[0:1, :],
                weight_ref[0:1, :],
                jnp.where(key == target_ref[1:2, :], weight_ref[1:2, :], 0.0),
            )
            scale = jnp.sum(spread, axis=1, keepdims=True)
            chosen = jnp.where(spread > 0.0, 1.0, 0.0).astype(jnp.bfloat16)
            picked = jnp.dot(chosen, tokens_ref[...], preferred_element_type=jnp.float32)
            sent = (picked * scale).astype(jnp.bfloat16)
            for g in range(group):
                for t in range(WIDE):
                    start = pl.multiple_of((i * group + g) * (WIDE * height) + t * height, 16)
                    send_ref[pl.ds(start, height), :] = sent[
                        g * height : (g + 1) * height, t * LANE : (t + 1) * LANE
                    ]
            return carry

        lax.fori_loop(0, experts // group, step, 0)

    return body


def split_state(replicas):
    def body(own_ref, *refs):
        inputs, outputs = refs[:3], refs[3:]
        for a in range(3):
            rows = inputs[a].shape[0]
            height = WIDE * rows + rows // 2
            for r in range(replicas):
                owner = own_ref[0] ^ r
                for t in range(WIDE):
                    start = pl.multiple_of(owner * SPAN + t * LANE, LANE)
                    outputs[r][a * height + t * rows : a * height + (t + 1) * rows, :] = inputs[a][
                        :, pl.ds(start, LANE)
                    ]
                start = pl.multiple_of(replicas * SPAN + (owner >> 1) * LANE, LANE)
                tile = inputs[a][:, pl.ds(start, LANE)].astype(jnp.float32)
                turned = pltpu.roll(tile, HALF, 1)
                odd = jnp.broadcast_to(owner & 1, (rows // 2, LANE)) == 1
                low = jnp.where(odd, turned[: rows // 2], tile[: rows // 2])
                high = jnp.where(odd, tile[rows // 2 :], turned[rows // 2 :])
                left = iota((rows // 2, LANE), 1) < HALF
                outputs[r][a * height + WIDE * rows : (a + 1) * height, :] = jnp.where(
                    left, low, high
                ).astype(jnp.bfloat16)

    return body


def split_tail(replicas):
    def body(own_ref, tail_ref, *refs):
        outputs, buffer_ref = refs[:replicas], refs[replicas]
        buffer_ref[...] = tail_ref[...].astype(jnp.float32)
        count = outputs[0].shape[0]
        for r in range(replicas):
            owner = own_ref[0] ^ r
            outputs[r][...] = buffer_ref[pl.ds(owner, count, stride=replicas), :].astype(
                jnp.bfloat16
            )

    return body


def order_hidden(experts, capacity, replicas, group):
    rows = group * capacity
    total = replicas * rows

    def body(*refs):
        pieces, out_ref = refs[:replicas], refs[replicas]
        source, replica, slot = digits(iota((total, total), 0), group, replicas, capacity)
        wanted = replica * rows + source * capacity + slot
        move = jnp.where(iota((total, total), 1) == wanted, 1.0, 0.0).astype(jnp.bfloat16)

        def step(i, carry):
            start = pl.multiple_of(i * rows, 16)
            stacked = jnp.concatenate([ref[pl.ds(start, rows), :] for ref in pieces], axis=0)
            moved = jnp.dot(move, stacked, preferred_element_type=jnp.float32)
            place = pl.multiple_of(i * total, LANE)
            out_ref[:, pl.ds(place, total)] = jnp.transpose(moved).astype(jnp.bfloat16)
            return carry

        lax.fori_loop(0, experts // group, step, 0)

    return body


def tail_gradient(capacity, replicas):
    half = capacity // 2

    def body(*refs):
        hidden_refs, tail_refs, out_ref = refs[:replicas], refs[replicas : 2 * replicas], refs[-1]
        folded = tail_refs[0].shape[0]
        rows = 2 * folded
        source, side, slot = digits(iota((rows, folded), 0), rows // capacity, 2, half)
        move = jnp.where(iota((rows, folded), 1) == source * half + slot, 1.0, 0.0)
        move = move.astype(jnp.bfloat16)
        side = digits(iota((rows, LANE), 0), rows // capacity, 2, half)[1]
        for r in range(replicas):
            moved = jnp.dot(move, tail_refs[r][...], preferred_element_type=jnp.float32)
            moved = jnp.where(side == 1, pltpu.roll(moved, HALF, 1), moved).astype(jnp.bfloat16)
            part = lax.dot_general(
                hidden_refs[r][0:rows, :],
                moved,
                (((0,), (0,)), ((), ())),
                preferred_element_type=jnp.float32,
            )
            if r == 0:
                out_ref[...] = part
            else:
                out_ref[...] += part

    return body


def finish(experts, capacity, replicas):
    height = replicas * capacity

    def body(own_ref, wide_ref, hidden_ref, tail_ref, *refs):
        state_refs, next_refs = refs[:replicas], refs[replicas : 2 * replicas]
        out_refs = refs[2 * replicas : 3 * replicas]
        gradient_ref, updated_ref = refs[3 * replicas :]
        rows = experts * height
        received = wide_ref[...].reshape(experts, WIDE * height, LANE)
        tiles = [
            received[:, t * height : (t + 1) * height, :].reshape(rows, LANE) for t in range(WIDE)
        ]
        gradient_ref[...] = jnp.dot(
            hidden_ref[...], jnp.concatenate(tiles, axis=1), preferred_element_type=jnp.float32
        )
        slab = state_refs[0].shape[0] * 2 // (3 * (2 * WIDE + 1))
        part = WIDE * slab + slab // 2
        for r in range(replicas):
            start = pl.multiple_of((own_ref[0] ^ r) * slab, slab)
            for t in range(WIDE):
                state = [
                    state_refs[r][a * part + t * slab : a * part + (t + 1) * slab, :]
                    for a in range(3)
                ]
                gradient = gradient_ref[pl.ds(start, slab), t * LANE : (t + 1) * LANE]
                updated_ref[pl.ds(start, slab), t * LANE : (t + 1) * LANE] = adamw(
                    *state, gradient
                )
            state = []
            for a in range(3):
                folded = state_refs[r][a * part + WIDE * slab : (a + 1) * part, :]
                folded = folded.astype(jnp.float32)
                state.append(jnp.concatenate([folded, pltpu.roll(folded, HALF, 1)], axis=0))
            updated_ref[pl.ds(start, slab), SPAN : SPAN + LANE] = adamw(
                *state, tail_ref[pl.ds(start, slab), :]
            )
        for r in range(replicas):
            out_refs[r][...] = jnp.dot(
                next_refs[r][...], updated_ref[...], preferred_element_type=jnp.float32
            ).astype(jnp.bfloat16)

    return body


def join_columns(replicas):
    def body(own_ref, *refs):
        pieces, out_ref = refs[:replicas], refs[replicas]
        rows = pieces[0].shape[0]
        left = iota((rows, LANE), 1) < HALF
        for r in range(replicas):
            owner = own_ref[0] ^ r
            start = pl.multiple_of(owner * SPAN, LANE)
            out_ref[:, pl.ds(start, SPAN)] = pieces[r][:, 0:SPAN]
            if r % 2 == 0:
                pair = [pieces[r + s][:, SPAN : SPAN + LANE].astype(jnp.float32) for s in (0, 1)]
                odd = jnp.broadcast_to(owner & 1, (rows, LANE)) == 1
                low = jnp.where(odd, pair[1], pair[0])
                high = pltpu.roll(jnp.where(odd, pair[0], pair[1]), HALF, 1)
                start = pl.multiple_of(replicas * SPAN + (owner >> 1) * LANE, LANE)
                out_ref[:, pl.ds(start, LANE)] = jnp.where(left, low, high).astype(jnp.bfloat16)

    return body


def per_device(
    out_grad,
    expert_ids,
    combine,
    router_logits,
    saved_hidden,
    weight,
    moment_one,
    moment_two,
    next_hidden,
    interpret=False,
):
    experts = lax.axis_size("ep")
    replicas = lax.axis_size("dp")
    rows_total = saved_hidden.shape[1]
    capacity = rows_total // experts
    tokens = out_grad.shape[0]
    slab_rows = weight.shape[1]
    ff_width = saved_hidden.shape[2]
    next_rows = next_hidden.shape[1]
    main = replicas * SPAN
    tail_rows = replicas * capacity // 2
    state_rows = 3 * (WIDE * slab_rows + slab_rows // 2)
    vmem = pl.BlockSpec(memory_space=pltpu.VMEM)
    smem = pl.BlockSpec(memory_space=pltpu.SMEM)
    own = lax.axis_index("dp").astype(jnp.int32).reshape(1)

    def call(body, ins, outs, scratch=(), scalar=False):
        shapes = [jax.ShapeDtypeStruct(shape, dtype) for shape, dtype in outs]
        single = len(shapes) == 1
        specs = [vmem] * len(ins)
        if scalar:
            specs, ins = [smem] + specs, [own] + list(ins)
        return pl.pallas_call(
            body,
            out_shape=shapes[0] if single else tuple(shapes),
            in_specs=specs,
            out_specs=vmem if single else (vmem,) * len(shapes),
            scratch_shapes=list(scratch),
            interpret=interpret,
        )(*ins)

    def exchange(pieces):
        return [pieces[0]] + [
            lax.ppermute(pieces[r], "dp", [(i, i ^ r) for i in range(replicas)])
            for r in range(1, replicas)
        ]

    def swap(value, parts):
        value = value.reshape(parts, value.shape[0] // parts, value.shape[1])
        value = lax.all_to_all(value, "ep", split_axis=0, concat_axis=0, tiled=True)
        return value.reshape(-1, value.shape[2])

    half16 = jnp.bfloat16
    ids_wide, combine_wide = expert_ids.T, combine.T
    message = call(
        own_block(replicas),
        [ids_wide, combine_wide, out_grad],
        [((tokens + META, SPAN), half16)] * replicas,
        scalar=True,
    )
    message = exchange(message)
    tail = call(
        own_tail(experts, capacity, replicas),
        [ids_wide, combine_wide, out_grad[:, main:]],
        [((experts * tail_rows, LANE), half16)],
    )
    tail = swap(tail, experts)
    send = call(
        own_columns(experts, capacity, replicas, tokens, 8),
        message,
        [((experts * WIDE * replicas * capacity, LANE), half16)],
        [
            pltpu.VMEM((replicas * tokens, SPAN), jnp.bfloat16),
            pltpu.VMEM((2, replicas * tokens), jnp.int32),
            pltpu.VMEM((2, replicas * tokens), jnp.float32),
        ],
    )
    wide = swap(send, experts)

    tail = call(
        split_tail(replicas),
        [tail],
        [((experts * capacity // 2, LANE), half16)] * replicas,
        [pltpu.VMEM((experts * tail_rows, LANE), jnp.float32)],
        scalar=True,
    )
    tail = exchange(tail)
    state = call(
        split_state(replicas),
        [weight[0], moment_one[0], moment_two[0]],
        [((state_rows, LANE), half16)] * replicas,
        scalar=True,
    )
    state = exchange(state)
    hidden = exchange([saved_hidden[0]] * replicas)
    following = exchange([next_hidden[0]] * replicas)

    gradient_tail = call(
        tail_gradient(capacity, replicas),
        hidden + tail,
        [((ff_width, LANE), jnp.float32)],
    )
    ordered = call(
        order_hidden(experts, capacity, replicas, 8),
        hidden,
        [((ff_width, replicas * rows_total), half16)],
    )
    result = call(
        finish(experts, capacity, replicas),
        [wide, ordered, gradient_tail] + state + following,
        [((next_rows, SPAN + LANE), half16)] * replicas,
        [
            pltpu.VMEM((ff_width, SPAN), jnp.float32),
            pltpu.VMEM((ff_width, SPAN + LANE), jnp.bfloat16),
        ],
        scalar=True,
    )
    result = exchange(result)
    refreshed = call(
        join_columns(replicas),
        result,
        [((next_rows, out_grad.shape[1]), half16)],
        scalar=True,
    )
    return (refreshed[None], zloss_grad(router_logits))


def solution(mesh):
    in_specs = (
        P(("ep", "dp"), None),
        P(("ep", "dp"), None),
        P(("ep", "dp"), None),
        P(("ep", "dp"), None),
        P("ep", "dp", None),
        P("ep", "dp", None),
        P("ep", "dp", None),
        P("ep", "dp", None),
        P("ep", "dp", None),
    )
    out_specs = (P("ep", "dp", None), P(("ep", "dp"), None))
    return jax.shard_map(
        per_device, mesh=mesh, in_specs=in_specs, out_specs=out_specs, check_vma=False
    )
```

```python
import jax
import jax.numpy as jnp
from jax import lax
from jax.experimental import pallas as pl
from jax.experimental.pallas import tpu as pltpu
from jax.sharding import PartitionSpec as P

beta_one = 0.9
beta_two = 0.95
learn_rate = 0.2
decay_rate = 0.1
step_count = 100.0
adam_eps = 1e-08
zloss_coef = 0.25

LANE = 128
HALF = 64
META = 8
WIDE = 3
SPAN = WIDE * LANE
SCOPED = 56 << 20


def adamw(weight, first, second, gradient):
    first_new = beta_one * first.astype(jnp.float32) + (1.0 - beta_one) * gradient
    second_new = beta_two * second.astype(jnp.float32) + (1.0 - beta_two) * gradient * gradient
    first_hat = first_new * (1.0 / (1.0 - beta_one**step_count))
    second_hat = second_new * (1.0 / (1.0 - beta_two**step_count))
    current = weight.astype(jnp.float32)
    change = first_hat / (jnp.sqrt(second_hat) + adam_eps) + decay_rate * current
    return (current - learn_rate * change).astype(jnp.bfloat16)


def zloss_grad(logits):
    values = logits.astype(jnp.float32)
    row_max = jnp.max(values, axis=-1, keepdims=True)
    log_total = row_max + jnp.log(jnp.sum(jnp.exp(values - row_max), axis=-1, keepdims=True))
    probs = jnp.exp(values - log_total)
    return (zloss_coef * 2.0 * log_total * probs).astype(jnp.bfloat16)


def iota(shape, dim):
    return lax.broadcasted_iota(jnp.int32, shape, dim)


def digits(value, *bases):
    found = []
    for base in reversed(bases):
        above = jnp.floor((value.astype(jnp.float32) + 0.5) * (1.0 / base)).astype(jnp.int32)
        found.append(value - above * base)
        value = above
    return found[::-1]


def slots_of(ids):
    tokens = ids[0].shape[1]
    wide = [jnp.broadcast_to(row, (tokens, tokens)) for row in ids]
    tall = [jnp.transpose(mat) for mat in wide]
    earlier = iota((tokens, tokens), 0) < iota((tokens, tokens), 1)
    counts = []
    for mat in wide:
        hits = jnp.where(earlier & (tall[0] == mat), 1.0, 0.0)
        hits = hits + jnp.where(earlier & (tall[1] == mat), 1.0, 0.0)
        counts.append(jnp.sum(hits, axis=0, keepdims=True))
    return counts


def own_block(replicas):
    def body(ids_ref, combine_ref, grad_ref, message_ref):
        ids = ids_ref[...].astype(jnp.float32)
        combine = combine_ref[...]
        tokens = ids.shape[1]
        fold = tokens // 2
        pieces = [ids[0:1], ids[1:2]]
        for k in range(2):
            rest = combine[k : k + 1]
            for _ in range(3):
                part = rest.astype(jnp.bfloat16).astype(jnp.float32)
                pieces.append(part)
                rest = rest - part
        meta = jnp.concatenate(pieces, axis=0).astype(jnp.bfloat16)
        left = iota((fold, LANE), 1) < HALF
        size = WIDE * tokens + fold + META
        for j in range(replicas):
            base = j * size
            for t in range(WIDE):
                column = j * SPAN + t * LANE
                message_ref[base + t * tokens : base + (t + 1) * tokens, :] = grad_ref[
                    :, column : column + LANE
                ]
            column = replicas * SPAN + (j // 2) * LANE
            tile = grad_ref[:, column : column + LANE].astype(jnp.float32)
            turned = pltpu.roll(tile, HALF, 1)
            if j % 2 == 0:
                folded = jnp.where(left, tile[:fold], turned[fold:])
            else:
                folded = jnp.where(left, turned[:fold], tile[fold:])
            base += WIDE * tokens
            message_ref[base : base + fold, :] = folded.astype(jnp.bfloat16)
            message_ref[base + fold : base + fold + META, :] = meta

    return body


def own_columns(experts, capacity, replicas, tokens, group):
    part = replicas // 2
    height = part * capacity
    fold = tokens // 2

    def body(message_ref, send_ref, tokens_ref, target_ref, weight_ref):
        size = WIDE * tokens + fold + META
        for j in range(replicas):
            base, row = j * size, j * tokens
            for t in range(WIDE):
                tokens_ref[row : row + tokens, t * LANE : (t + 1) * LANE] = message_ref[
                    base + t * tokens : base + (t + 1) * tokens, :
                ]
            base += WIDE * tokens
            folded = message_ref[base : base + fold, :]
            turned = pltpu.roll(folded.astype(jnp.float32), HALF, 1).astype(jnp.bfloat16)
            tokens_ref[row : row + fold, SPAN : SPAN + LANE] = folded
            tokens_ref[row + fold : row + tokens, SPAN : SPAN + LANE] = turned
            meta = message_ref[base + fold : base + fold + META, 0:tokens].astype(jnp.float32)
            id_rows = [meta[0:1], meta[1:2]]
            slots = slots_of(id_rows)
            for k in range(2):
                where = id_rows[k] * height + slots[k] + float((j % part) * capacity)
                target_ref[k : k + 1, row : row + tokens] = where.astype(jnp.int32)
                first = 2 + 3 * k
                weight_ref[k : k + 1, row : row + tokens] = (
                    meta[first : first + 1] + meta[first + 1 : first + 2]
                ) + meta[first + 2 : first + 3]
        rows = group * height
        block = part * tokens
        total = 2 * WIDE * height + height
        left = iota((height, LANE), 1) < HALF

        def step(i, carry):
            key = iota((rows, block), 0) + i * rows
            lasts = []
            for h in range(2):
                columns = slice(h * block, (h + 1) * block)
                spread = jnp.where(
                    key == target_ref[0:1, columns],
                    weight_ref[0:1, columns],
                    jnp.where(key == target_ref[1:2, columns], weight_ref[1:2, columns], 0.0),
                )
                scale = jnp.sum(spread, axis=1, keepdims=True)
                chosen = jnp.where(spread > 0.0, 1.0, 0.0).astype(jnp.bfloat16)
                picked = jnp.dot(
                    chosen, tokens_ref[columns, :], preferred_element_type=jnp.float32
                )
                sent = picked * scale
                for g in range(group):
                    for t in range(WIDE):
                        start = (i * group + g) * total + (h * WIDE + t) * height
                        send_ref[pl.ds(pl.multiple_of(start, 8), height), :] = sent[
                            g * height : (g + 1) * height, t * LANE : (t + 1) * LANE
                        ].astype(jnp.bfloat16)
                lasts.append(sent[:, SPAN : SPAN + LANE])
            turned = pltpu.roll(lasts[1], HALF, 1)
            for g in range(group):
                place = slice(g * height, (g + 1) * height)
                start = (i * group + g) * total + 2 * WIDE * height
                send_ref[pl.ds(pl.multiple_of(start, 8), height), :] = jnp.where(
                    left, lasts[0][place], turned[place]
                ).astype(jnp.bfloat16)
            return carry

        lax.fori_loop(0, experts // group, step, 0)

    return body


def split_state(replicas):
    def body(own_ref, *refs):
        inputs, outputs = refs[:3], refs[3:]
        for a in range(3):
            rows = inputs[a].shape[0]
            height = WIDE * rows + rows // 2
            for r in range(replicas):
                owner = own_ref[0] ^ r
                for t in range(WIDE):
                    start = pl.multiple_of(owner * SPAN + t * LANE, LANE)
                    outputs[r][a * height + t * rows : a * height + (t + 1) * rows, :] = inputs[a][
                        :, pl.ds(start, LANE)
                    ]
                start = pl.multiple_of(replicas * SPAN + (owner >> 1) * LANE, LANE)
                tile = inputs[a][:, pl.ds(start, LANE)].astype(jnp.float32)
                turned = pltpu.roll(tile, HALF, 1)
                odd = jnp.broadcast_to(owner & 1, (rows // 2, LANE)) == 1
                low = jnp.where(odd, turned[: rows // 2], tile[: rows // 2])
                high = jnp.where(odd, tile[rows // 2 :], turned[rows // 2 :])
                left = iota((rows // 2, LANE), 1) < HALF
                outputs[r][a * height + WIDE * rows : (a + 1) * height, :] = jnp.where(
                    left, low, high
                ).astype(jnp.bfloat16)

    return body


def order_hidden(experts, capacity, replicas, group):
    rows = group * capacity
    part = replicas // 2
    total = part * rows
    runs = 2

    def body(own_ref, *refs):
        pieces, out_ref = refs[:replicas], refs[replicas]
        units = out_ref.shape[1]
        half, source, replica, slot = digits(iota((2 * total, 2 * total), 0), 2, group, part, capacity)
        origin = (half * part + replica) ^ own_ref[0]
        wanted = origin * rows + source * capacity + slot
        move = jnp.where(iota((2 * total, 2 * total), 1) == wanted, 1.0, 0.0)
        move = move.astype(jnp.bfloat16)
        steps = experts // group
        for i in range(steps):
            stacked = jnp.concatenate(
                [ref[i * rows : (i + 1) * rows, :] for ref in pieces], axis=0
            )
            moved = jnp.dot(move, stacked, preferred_element_type=jnp.float32)
            moved = jnp.transpose(moved).astype(jnp.bfloat16)
            run, place = i // (steps // runs), i % (steps // runs)
            for h in range(2):
                out_ref[2 * run + h, :, place * total : (place + 1) * total] = moved[
                    :, h * total : (h + 1) * total
                ]

    return body


def finish(experts, capacity, replicas, far):
    part = replicas // 2
    height = part * capacity
    runs = 2

    def body(own_ref, wide_ref, hidden_ref, *refs):
        state_hbm, next_hbm = refs[:replicas], refs[replicas : 2 * replicas]
        out_ref, units_ref, state_ref, next_ref, gradient_ref, updated_ref, sems = refs[
            2 * replicas :
        ]
        total = wide_ref.shape[0] // experts
        run_rows = experts // runs * total
        state_rows = state_hbm[0].shape[0]
        rows = next_hbm[0].shape[0] - far
        count = experts // runs * height
        copies = [
            pltpu.make_async_copy(hidden_ref.at[i], units_ref.at[i], sems.at[i])
            for i in range(2 * runs)
        ]
        for r in range(replicas):
            place = pl.ds(r * state_rows, state_rows)
            copies.append(
                pltpu.make_async_copy(
                    state_hbm[r], state_ref.at[place], sems.at[2 * runs + r]
                )
            )
        for r in range(replicas):
            copies.append(
                pltpu.make_async_copy(
                    next_hbm[r].at[pl.ds(far, rows)],
                    next_ref.at[pl.ds(r * rows, rows)],
                    sems.at[2 * runs + replicas + r],
                )
            )
        for copy in copies:
            copy.start()
        for run in range(runs):
            received = wide_ref[run * run_rows : (run + 1) * run_rows, :]
            received = received.reshape(experts // runs, total, LANE)
            last = received[:, 2 * WIDE * height : total, :].reshape(count, LANE)
            for h in range(2):
                tiles = [
                    received[:, (h * WIDE + t) * height : (h * WIDE + t + 1) * height, :].reshape(
                        count, LANE
                    )
                    for t in range(WIDE)
                ]
                copies[2 * run + h].wait()
                product = jnp.dot(
                    units_ref[2 * run + h],
                    jnp.concatenate(tiles + [last], axis=1),
                    preferred_element_type=jnp.float32,
                )
                if h == 1:
                    turned = pltpu.roll(product[:, SPAN : SPAN + LANE], HALF, 1)
                    product = jnp.concatenate([product[:, :SPAN], turned], axis=1)
                if run == 0 and h == 0:
                    gradient_ref[...] = product
                else:
                    gradient_ref[...] += product
        slab = state_rows * 2 // (3 * (2 * WIDE + 1))
        piece = WIDE * slab + slab // 2
        for r in range(replicas):
            copies[2 * runs + r].wait()
            start = pl.multiple_of((own_ref[0] ^ r) * slab, slab)
            for t in range(WIDE + 1):
                state = []
                for a in range(3):
                    base = r * state_rows + a * piece + t * slab
                    if t < WIDE:
                        state.append(state_ref[base : base + slab, :])
                    else:
                        folded = state_ref[base : base + slab // 2, :].astype(jnp.float32)
                        state.append(
                            jnp.concatenate([folded, pltpu.roll(folded, HALF, 1)], axis=0)
                        )
                gradient = gradient_ref[pl.ds(start, slab), t * LANE : (t + 1) * LANE]
                updated_ref[pl.ds(start, slab), t * LANE : (t + 1) * LANE] = adamw(
                    *state, gradient
                )
        for copy in copies[2 * runs + replicas :]:
            copy.wait()
        result = jnp.dot(next_ref[...], updated_ref[...], preferred_element_type=jnp.float32)
        for r in range(replicas):
            start = pl.multiple_of((own_ref[0] ^ r) * rows, 16)
            out_ref[pl.ds(start, rows), :] = result[r * rows : (r + 1) * rows, :].astype(
                jnp.bfloat16
            )

    return body


def join_columns(replicas):
    def body(pieces_ref, out_ref):
        rows = out_ref.shape[0]
        left = iota((rows, LANE), 1) < HALF
        for j in range(replicas):
            out_ref[:, j * SPAN : (j + 1) * SPAN] = pieces_ref[j * rows : (j + 1) * rows, 0:SPAN]
            if j % 2 == 0:
                low, high = [
                    pieces_ref[(j + s) * rows : (j + s + 1) * rows, SPAN : SPAN + LANE].astype(
                        jnp.float32
                    )
                    for s in (0, 1)
                ]
                start = replicas * SPAN + (j // 2) * LANE
                out_ref[:, start : start + LANE] = jnp.where(
                    left, low, pltpu.roll(high, HALF, 1)
                ).astype(jnp.bfloat16)

    return body


def per_device(
    out_grad,
    expert_ids,
    combine,
    router_logits,
    saved_hidden,
    weight,
    moment_one,
    moment_two,
    next_hidden,
    interpret=False,
):
    experts = lax.axis_size("ep")
    replicas = lax.axis_size("dp")
    rows_total = saved_hidden.shape[1]
    capacity = rows_total // experts
    tokens = out_grad.shape[0]
    slab_rows = weight.shape[1]
    ff_width = saved_hidden.shape[2]
    next_rows = next_hidden.shape[1]
    part = replicas // 2
    message_rows = WIDE * tokens + tokens // 2 + META
    expert_rows = (2 * WIDE + 1) * part * capacity
    state_rows = 3 * (WIDE * slab_rows + slab_rows // 2)
    vmem = pl.BlockSpec(memory_space=pltpu.VMEM)
    smem = pl.BlockSpec(memory_space=pltpu.SMEM)
    hbm = pl.BlockSpec(memory_space=pl.ANY)
    own = lax.axis_index("dp").astype(jnp.int32).reshape(1)

    def near(value):
        return value if interpret else pltpu.with_memory_space_constraint(value, pltpu.VMEM)

    def call(body, ins, outs, scratch=(), scalar=False, local=False, last=False, specs=None):
        kind = pltpu.VMEM if local and not interpret and not last else jax.ShapeDtypeStruct
        shapes = [kind(shape, dtype) for shape, dtype in outs]
        single = len(shapes) == 1
        specs = specs or [vmem] * len(ins)
        if scalar:
            specs, ins = [smem] + specs, [own] + list(ins)
        return pl.pallas_call(
            body,
            out_shape=shapes[0] if single else tuple(shapes),
            in_specs=specs,
            out_specs=vmem if single else (vmem,) * len(shapes),
            scratch_shapes=list(scratch),
            compiler_params=pltpu.CompilerParams(vmem_limit_bytes=SCOPED if local else None),
            interpret=interpret,
        )(*ins)

    def send(value, r):
        return lax.ppermute(value, "dp", [(i, i ^ r) for i in range(replicas)])

    def tie(*values):
        return lax.optimization_barrier(values)

    def spread(value, pieces):
        if part != 4:
            return (
                [value] + [send(value, r) for r in range(1, replicas)],
                pieces[:1] + [send(pieces[r], r) for r in range(1, replicas)],
            )
        moved = {r: send(pieces[r], r) for r in (1, 3)}
        first = (send(value, 1), send(value, 3), send(value, part), moved[1], moved[3])
        near1, near3, far0, moved[1], moved[3], *pieces = tie(*first, *pieces)
        moved[4] = send(pieces[4], 4)
        far1, far3, near3, moved[4], *pieces = tie(
            send(far0, 1), send(far0, 3), near3, moved[4], *pieces
        )
        moved[2] = send(pieces[2], 2)
        near2, far2, moved[2], *pieces = tie(send(near3, 1), send(far1, 3), moved[2], *pieces)
        moved.update({r: send(pieces[r], r) for r in (6, 5, 7)})
        gathered = [value, near1, near2, near3, far0, far1, far2, far3]
        return gathered, pieces[:1] + [moved[r] for r in range(1, replicas)]

    def swap(value, axis):
        parts = lax.axis_size(axis)
        value = value.reshape(parts, value.shape[0] // parts, value.shape[1])
        value = lax.all_to_all(value, axis, split_axis=0, concat_axis=0, tiled=True)
        return value.reshape(-1, value.shape[2])

    half16 = jnp.bfloat16
    message = call(
        own_block(replicas),
        [expert_ids.T, combine.T, out_grad],
        [((replicas * message_rows, LANE), half16)],
        local=True,
    )
    message = swap(message, "dp")
    hidden = jnp.concatenate([saved_hidden[0], next_hidden[0]], axis=0)
    state = call(
        split_state(replicas),
        [weight[0], moment_one[0], moment_two[0]],
        [((state_rows, LANE), half16)] * replicas,
        scalar=True,
    )
    message, hidden, *state = tie(message, hidden, *state)
    wide = call(
        own_columns(experts, capacity, replicas, tokens, 8),
        [near(message)],
        [((experts * expert_rows, LANE), half16)],
        [
            pltpu.VMEM((replicas * tokens, SPAN + LANE), half16),
            pltpu.VMEM((2, replicas * tokens), jnp.int32),
            pltpu.VMEM((2, replicas * tokens), jnp.float32),
        ],
        local=True,
    )
    wide = swap(wide, "ep")
    hidden, state = spread(hidden, state)

    runs = 2
    ordered = call(
        order_hidden(experts, capacity, replicas, 8),
        hidden,
        [((2 * runs, ff_width, part * rows_total // runs), half16)],
        scalar=True,
    )
    result = call(
        finish(experts, capacity, replicas, rows_total),
        [near(wide), ordered] + state + hidden,
        [((replicas * next_rows, SPAN + LANE), half16)],
        [
            pltpu.VMEM((2 * runs, ff_width, part * rows_total // runs), half16),
            pltpu.VMEM((replicas * state_rows, LANE), half16),
            pltpu.VMEM((replicas * next_rows, ff_width), half16),
            pltpu.VMEM((ff_width, SPAN + LANE), jnp.float32),
            pltpu.VMEM((ff_width, SPAN + LANE), half16),
            pltpu.SemaphoreType.DMA((2 * runs + 2 * replicas,)),
        ],
        scalar=True,
        local=True,
        specs=[vmem] + [hbm] * (1 + 2 * replicas),
    )
    result = swap(result, "dp")
    refreshed = call(
        join_columns(replicas),
        [near(result)],
        [((next_rows, out_grad.shape[1]), half16)],
        local=True,
        last=True,
    )
    return (refreshed[None], zloss_grad(router_logits))


def solution(mesh):
    in_specs = (
        P(("ep", "dp"), None),
        P(("ep", "dp"), None),
        P(("ep", "dp"), None),
        P(("ep", "dp"), None),
        P("ep", "dp", None),
        P("ep", "dp", None),
        P("ep", "dp", None),
        P("ep", "dp", None),
        P("ep", "dp", None),
    )
    out_specs = (P("ep", "dp", None), P(("ep", "dp"), None))
    return jax.shard_map(
        per_device, mesh=mesh, in_specs=in_specs, out_specs=out_specs, check_vma=False
    )
```

```python
import jax
import jax.numpy as jnp
from jax import lax
from jax.experimental import pallas as pl
from jax.experimental.pallas import tpu as pltpu
from jax.sharding import PartitionSpec as P

beta_one = 0.9
beta_two = 0.95
learn_rate = 0.2
decay_rate = 0.1
step_count = 100.0
adam_eps = 1e-08
zloss_coef = 0.25

LANE = 128
HALF = 64
META = 8
WIDE = 3
SPAN = WIDE * LANE
SCOPED = 56 << 20


def adamw(weight, first, second, gradient):
    first_new = beta_one * first.astype(jnp.float32) + (1.0 - beta_one) * gradient
    second_new = beta_two * second.astype(jnp.float32) + (1.0 - beta_two) * gradient * gradient
    first_hat = first_new * (1.0 / (1.0 - beta_one**step_count))
    second_hat = second_new * (1.0 / (1.0 - beta_two**step_count))
    current = weight.astype(jnp.float32)
    change = first_hat / (jnp.sqrt(second_hat) + adam_eps) + decay_rate * current
    return (current - learn_rate * change).astype(jnp.bfloat16)


def zloss_grad(logits):
    values = logits.astype(jnp.float32)
    row_max = jnp.max(values, axis=-1, keepdims=True)
    log_total = row_max + jnp.log(jnp.sum(jnp.exp(values - row_max), axis=-1, keepdims=True))
    probs = jnp.exp(values - log_total)
    return (zloss_coef * 2.0 * log_total * probs).astype(jnp.bfloat16)


def iota(shape, dim):
    return lax.broadcasted_iota(jnp.int32, shape, dim)


def digits(value, *bases):
    found = []
    for base in reversed(bases):
        above = jnp.floor((value.astype(jnp.float32) + 0.5) * (1.0 / base)).astype(jnp.int32)
        found.append(value - above * base)
        value = above
    return found[::-1]


def slots_of(ids):
    tokens = ids[0].shape[1]
    wide = [jnp.broadcast_to(row, (tokens, tokens)) for row in ids]
    tall = [jnp.transpose(mat) for mat in wide]
    earlier = iota((tokens, tokens), 0) < iota((tokens, tokens), 1)
    counts = []
    for mat in wide:
        hits = jnp.where(earlier & (tall[0] == mat), 1.0, 0.0)
        hits = hits + jnp.where(earlier & (tall[1] == mat), 1.0, 0.0)
        counts.append(jnp.sum(hits, axis=0, keepdims=True))
    return counts


def own_block(replicas):
    def body(ids_ref, combine_ref, grad_ref, message_ref):
        ids = ids_ref[...].astype(jnp.float32)
        combine = combine_ref[...]
        tokens = ids.shape[1]
        fold = tokens // 2
        pieces = [ids[0:1], ids[1:2]]
        for k in range(2):
            rest = combine[k : k + 1]
            for _ in range(3):
                part = rest.astype(jnp.bfloat16).astype(jnp.float32)
                pieces.append(part)
                rest = rest - part
        meta = jnp.concatenate(pieces, axis=0).astype(jnp.bfloat16)
        left = iota((fold, LANE), 1) < HALF
        size = WIDE * tokens + fold + META
        for j in range(replicas):
            base = j * size
            for t in range(WIDE):
                column = j * SPAN + t * LANE
                message_ref[base + t * tokens : base + (t + 1) * tokens, :] = grad_ref[
                    :, column : column + LANE
                ]
            column = replicas * SPAN + (j // 2) * LANE
            tile = grad_ref[:, column : column + LANE].astype(jnp.float32)
            turned = pltpu.roll(tile, HALF, 1)
            if j % 2 == 0:
                folded = jnp.where(left, tile[:fold], turned[fold:])
            else:
                folded = jnp.where(left, turned[:fold], tile[fold:])
            base += WIDE * tokens
            message_ref[base : base + fold, :] = folded.astype(jnp.bfloat16)
            message_ref[base + fold : base + fold + META, :] = meta

    return body


def own_columns(experts, capacity, replicas, tokens, group):
    part = replicas // 2
    height = part * capacity
    fold = tokens // 2

    def body(message_ref, send_ref, tokens_ref, target_ref, weight_ref):
        size = WIDE * tokens + fold + META
        for j in range(replicas):
            base, row = j * size, j * tokens
            for t in range(WIDE):
                tokens_ref[row : row + tokens, t * LANE : (t + 1) * LANE] = message_ref[
                    base + t * tokens : base + (t + 1) * tokens, :
                ]
            base += WIDE * tokens
            folded = message_ref[base : base + fold, :]
            turned = pltpu.roll(folded.astype(jnp.float32), HALF, 1).astype(jnp.bfloat16)
            tokens_ref[row : row + fold, SPAN : SPAN + LANE] = folded
            tokens_ref[row + fold : row + tokens, SPAN : SPAN + LANE] = turned
            meta = message_ref[base + fold : base + fold + META, 0:tokens].astype(jnp.float32)
            id_rows = [meta[0:1], meta[1:2]]
            slots = slots_of(id_rows)
            for k in range(2):
                where = id_rows[k] * height + slots[k] + float((j % part) * capacity)
                target_ref[k : k + 1, row : row + tokens] = where.astype(jnp.int32)
                first = 2 + 3 * k
                weight_ref[k : k + 1, row : row + tokens] = (
                    meta[first : first + 1] + meta[first + 1 : first + 2]
                ) + meta[first + 2 : first + 3]
        rows = group * height
        block = part * tokens
        total = 2 * WIDE * height + height
        left = iota((height, LANE), 1) < HALF

        def step(i, carry):
            key = iota((rows, block), 0) + i * rows
            lasts = []
            for h in range(2):
                columns = slice(h * block, (h + 1) * block)
                spread = jnp.where(
                    key == target_ref[0:1, columns],
                    weight_ref[0:1, columns],
                    jnp.where(key == target_ref[1:2, columns], weight_ref[1:2, columns], 0.0),
                )
                scale = jnp.sum(spread, axis=1, keepdims=True)
                chosen = jnp.where(spread > 0.0, 1.0, 0.0).astype(jnp.bfloat16)
                picked = jnp.dot(
                    chosen, tokens_ref[columns, :], preferred_element_type=jnp.float32
                )
                sent = picked * scale
                for g in range(group):
                    for t in range(WIDE):
                        start = (i * group + g) * total + (h * WIDE + t) * height
                        send_ref[pl.ds(pl.multiple_of(start, 8), height), :] = sent[
                            g * height : (g + 1) * height, t * LANE : (t + 1) * LANE
                        ].astype(jnp.bfloat16)
                lasts.append(sent[:, SPAN : SPAN + LANE])
            turned = pltpu.roll(lasts[1], HALF, 1)
            for g in range(group):
                place = slice(g * height, (g + 1) * height)
                start = (i * group + g) * total + 2 * WIDE * height
                send_ref[pl.ds(pl.multiple_of(start, 8), height), :] = jnp.where(
                    left, lasts[0][place], turned[place]
                ).astype(jnp.bfloat16)
            return carry

        lax.fori_loop(0, experts // group, step, 0)

    return body


def split_state(replicas):
    def body(own_ref, *refs):
        inputs, outputs = refs[:3], list(refs[3:])
        part = replicas // 2
        size = outputs[0].shape[0]
        outputs += [outputs[part].at[pl.ds(r * size, size)] for r in range(1, part)]
        for a in range(3):
            rows = inputs[a].shape[0]
            height = WIDE * rows + rows // 2
            for r in range(replicas):
                owner = own_ref[0] ^ r
                for t in range(WIDE):
                    start = pl.multiple_of(owner * SPAN + t * LANE, LANE)
                    outputs[r][a * height + t * rows : a * height + (t + 1) * rows, :] = inputs[a][
                        :, pl.ds(start, LANE)
                    ]
                start = pl.multiple_of(replicas * SPAN + (owner >> 1) * LANE, LANE)
                tile = inputs[a][:, pl.ds(start, LANE)].astype(jnp.float32)
                turned = pltpu.roll(tile, HALF, 1)
                odd = jnp.broadcast_to(owner & 1, (rows // 2, LANE)) == 1
                low = jnp.where(odd, turned[: rows // 2], tile[: rows // 2])
                high = jnp.where(odd, tile[rows // 2 :], turned[rows // 2 :])
                left = iota((rows // 2, LANE), 1) < HALF
                outputs[r][a * height + WIDE * rows : (a + 1) * height, :] = jnp.where(
                    left, low, high
                ).astype(jnp.bfloat16)

    return body


def order_hidden(experts, capacity, replicas, group):
    rows = group * capacity
    part = replicas // 2
    total = part * rows
    runs = 2

    def body(own_ref, *refs):
        pieces, out_ref = refs[:replicas], refs[replicas]
        units = out_ref.shape[1]
        half, source, replica, slot = digits(iota((2 * total, 2 * total), 0), 2, group, part, capacity)
        origin = (half * part + replica) ^ own_ref[0]
        wanted = origin * rows + source * capacity + slot
        move = jnp.where(iota((2 * total, 2 * total), 1) == wanted, 1.0, 0.0)
        move = move.astype(jnp.bfloat16)
        steps = experts // group
        for i in range(steps):
            stacked = jnp.concatenate(
                [ref[i * rows : (i + 1) * rows, :] for ref in pieces], axis=0
            )
            moved = jnp.dot(move, stacked, preferred_element_type=jnp.float32)
            moved = jnp.transpose(moved).astype(jnp.bfloat16)
            run, place = i // (steps // runs), i % (steps // runs)
            for h in range(2):
                out_ref[2 * run + h, :, place * total : (place + 1) * total] = moved[
                    :, h * total : (h + 1) * total
                ]

    return body


def finish(experts, capacity, replicas, far):
    part = replicas // 2
    height = part * capacity
    runs = 2

    def body(own_ref, wide_ref, hidden_ref, *refs):
        state_hbm, next_hbm = refs[:replicas], refs[replicas : 2 * replicas]
        out_ref, units_ref, state_ref, next_ref, gradient_ref, updated_ref, sems = refs[
            2 * replicas :
        ]
        total = wide_ref.shape[0] // experts
        run_rows = experts // runs * total
        state_rows = state_hbm[0].shape[0]
        rows = next_hbm[0].shape[0] - far
        count = experts // runs * height
        copies = [
            pltpu.make_async_copy(hidden_ref.at[i], units_ref.at[i], sems.at[i])
            for i in range(2 * runs)
        ]
        for r in range(replicas):
            place = pl.ds(r * state_rows, state_rows)
            copies.append(
                pltpu.make_async_copy(
                    state_hbm[r], state_ref.at[place], sems.at[2 * runs + r]
                )
            )
        for r in range(replicas):
            copies.append(
                pltpu.make_async_copy(
                    next_hbm[r].at[pl.ds(far, rows)],
                    next_ref.at[pl.ds(r * rows, rows)],
                    sems.at[2 * runs + replicas + r],
                )
            )
        for copy in copies:
            copy.start()
        for run in range(runs):
            received = wide_ref[run * run_rows : (run + 1) * run_rows, :]
            received = received.reshape(experts // runs, total, LANE)
            last = received[:, 2 * WIDE * height : total, :].reshape(count, LANE)
            for h in range(2):
                tiles = [
                    received[:, (h * WIDE + t) * height : (h * WIDE + t + 1) * height, :].reshape(
                        count, LANE
                    )
                    for t in range(WIDE)
                ]
                copies[2 * run + h].wait()
                product = jnp.dot(
                    units_ref[2 * run + h],
                    jnp.concatenate(tiles + [last], axis=1),
                    preferred_element_type=jnp.float32,
                )
                if h == 1:
                    turned = pltpu.roll(product[:, SPAN : SPAN + LANE], HALF, 1)
                    product = jnp.concatenate([product[:, :SPAN], turned], axis=1)
                if run == 0 and h == 0:
                    gradient_ref[...] = product
                else:
                    gradient_ref[...] += product
        slab = state_rows * 2 // (3 * (2 * WIDE + 1))
        piece = WIDE * slab + slab // 2
        for r in range(replicas):
            copies[2 * runs + r].wait()
            start = pl.multiple_of((own_ref[0] ^ r) * slab, slab)
            for t in range(WIDE + 1):
                state = []
                for a in range(3):
                    base = r * state_rows + a * piece + t * slab
                    if t < WIDE:
                        state.append(state_ref[base : base + slab, :])
                    else:
                        folded = state_ref[base : base + slab // 2, :].astype(jnp.float32)
                        state.append(
                            jnp.concatenate([folded, pltpu.roll(folded, HALF, 1)], axis=0)
                        )
                gradient = gradient_ref[pl.ds(start, slab), t * LANE : (t + 1) * LANE]
                updated_ref[pl.ds(start, slab), t * LANE : (t + 1) * LANE] = adamw(
                    *state, gradient
                )
        for copy in copies[2 * runs + replicas :]:
            copy.wait()
        result = jnp.dot(next_ref[...], updated_ref[...], preferred_element_type=jnp.float32)
        for r in range(replicas):
            start = pl.multiple_of((own_ref[0] ^ r) * rows, 16)
            out_ref[pl.ds(start, rows), :] = result[r * rows : (r + 1) * rows, :].astype(
                jnp.bfloat16
            )

    return body


def join_columns(replicas):
    def body(pieces_ref, out_ref):
        rows = out_ref.shape[0]
        left = iota((rows, LANE), 1) < HALF
        for j in range(replicas):
            out_ref[:, j * SPAN : (j + 1) * SPAN] = pieces_ref[j * rows : (j + 1) * rows, 0:SPAN]
            if j % 2 == 0:
                low, high = [
                    pieces_ref[(j + s) * rows : (j + s + 1) * rows, SPAN : SPAN + LANE].astype(
                        jnp.float32
                    )
                    for s in (0, 1)
                ]
                start = replicas * SPAN + (j // 2) * LANE
                out_ref[:, start : start + LANE] = jnp.where(
                    left, low, pltpu.roll(high, HALF, 1)
                ).astype(jnp.bfloat16)

    return body


def per_device(
    out_grad,
    expert_ids,
    combine,
    router_logits,
    saved_hidden,
    weight,
    moment_one,
    moment_two,
    next_hidden,
    interpret=False,
):
    experts = lax.axis_size("ep")
    replicas = lax.axis_size("dp")
    rows_total = saved_hidden.shape[1]
    capacity = rows_total // experts
    tokens = out_grad.shape[0]
    slab_rows = weight.shape[1]
    ff_width = saved_hidden.shape[2]
    next_rows = next_hidden.shape[1]
    part = replicas // 2
    message_rows = WIDE * tokens + tokens // 2 + META
    expert_rows = (2 * WIDE + 1) * part * capacity
    state_rows = 3 * (WIDE * slab_rows + slab_rows // 2)
    vmem = pl.BlockSpec(memory_space=pltpu.VMEM)
    smem = pl.BlockSpec(memory_space=pltpu.SMEM)
    hbm = pl.BlockSpec(memory_space=pl.ANY)
    own = lax.axis_index("dp").astype(jnp.int32).reshape(1)

    def near(value):
        return value if interpret else pltpu.with_memory_space_constraint(value, pltpu.VMEM)

    def call(body, ins, outs, scratch=(), scalar=False, local=False, last=False, specs=None):
        kind = pltpu.VMEM if local and not interpret and not last else jax.ShapeDtypeStruct
        shapes = [kind(shape, dtype) for shape, dtype in outs]
        single = len(shapes) == 1
        specs = specs or [vmem] * len(ins)
        if scalar:
            specs, ins = [smem] + specs, [own] + list(ins)
        return pl.pallas_call(
            body,
            out_shape=shapes[0] if single else tuple(shapes),
            in_specs=specs,
            out_specs=vmem if single else (vmem,) * len(shapes),
            scratch_shapes=list(scratch),
            compiler_params=pltpu.CompilerParams(vmem_limit_bytes=SCOPED if local else None),
            interpret=interpret,
        )(*ins)

    def send(value, r):
        return lax.ppermute(value, "dp", [(i, i ^ r) for i in range(replicas)])

    def tie(*values):
        return lax.optimization_barrier(values)

    def spread(value, pieces, across):
        if part != 4:
            return [value, send(value, part)], [pieces[0], send(across, part)]
        first = (send(value, part), send(value, 1), send(value, 3))
        moved = {r: send(pieces[r], r) for r in (1, 3)}
        far0, near1, near3, moved[1], moved[3], across, last = tie(
            *first, moved[1], moved[3], across, pieces[2]
        )
        far1, far3, across = send(far0, 1), send(far0, 3), send(across, part)
        far1, far3, near3, last = tie(far1, far3, near3, last)
        far2, near2 = send(far1, 3), send(near3, 1)
        far2, near2, across, last = tie(far2, near2, across, last)
        across = [across[q * state_rows : (q + 1) * state_rows] for q in range(part)]
        moved.update({0: pieces[0], 2: send(last, 2), 4: across[0]})
        moved.update({part + q: send(across[q], q) for q in (1, 3, 2)})
        gathered = [value, near1, near2, near3, far0, far1, far2, far3]
        return gathered, [moved[r] for r in range(replicas)]

    def swap(value, axis):
        parts = lax.axis_size(axis)
        value = value.reshape(parts, value.shape[0] // parts, value.shape[1])
        value = lax.all_to_all(value, axis, split_axis=0, concat_axis=0, tiled=True)
        return value.reshape(-1, value.shape[2])

    half16 = jnp.bfloat16
    message = call(
        own_block(replicas),
        [expert_ids.T, combine.T, out_grad],
        [((replicas * message_rows, LANE), half16)],
        local=True,
    )
    message = swap(message, "dp")
    hidden = jnp.concatenate([saved_hidden[0], next_hidden[0]], axis=0)
    state = call(
        split_state(replicas),
        [weight[0], moment_one[0], moment_two[0]],
        [((state_rows, LANE), half16)] * part + [((part * state_rows, LANE), half16)],
        scalar=True,
    )
    message, hidden, *state = tie(message, hidden, *state)
    wide = call(
        own_columns(experts, capacity, replicas, tokens, 8),
        [near(message)],
        [((experts * expert_rows, LANE), half16)],
        [
            pltpu.VMEM((replicas * tokens, SPAN + LANE), half16),
            pltpu.VMEM((2, replicas * tokens), jnp.int32),
            pltpu.VMEM((2, replicas * tokens), jnp.float32),
        ],
        local=True,
    )
    wide = swap(wide, "ep")
    hidden, state = spread(hidden, state[:part], state[part])

    runs = 2
    ordered = call(
        order_hidden(experts, capacity, replicas, 8),
        hidden,
        [((2 * runs, ff_width, part * rows_total // runs), half16)],
        scalar=True,
    )
    result = call(
        finish(experts, capacity, replicas, rows_total),
        [near(wide), ordered] + state + hidden,
        [((replicas * next_rows, SPAN + LANE), half16)],
        [
            pltpu.VMEM((2 * runs, ff_width, part * rows_total // runs), half16),
            pltpu.VMEM((replicas * state_rows, LANE), half16),
            pltpu.VMEM((replicas * next_rows, ff_width), half16),
            pltpu.VMEM((ff_width, SPAN + LANE), jnp.float32),
            pltpu.VMEM((ff_width, SPAN + LANE), half16),
            pltpu.SemaphoreType.DMA((2 * runs + 2 * replicas,)),
        ],
        scalar=True,
        local=True,
        specs=[vmem] + [hbm] * (1 + 2 * replicas),
    )
    result = swap(result, "dp")
    refreshed = call(
        join_columns(replicas),
        [near(result)],
        [((next_rows, out_grad.shape[1]), half16)],
        local=True,
        last=True,
    )
    return (refreshed[None], zloss_grad(router_logits))


def solution(mesh):
    in_specs = (
        P(("ep", "dp"), None),
        P(("ep", "dp"), None),
        P(("ep", "dp"), None),
        P(("ep", "dp"), None),
        P("ep", "dp", None),
        P("ep", "dp", None),
        P("ep", "dp", None),
        P("ep", "dp", None),
        P("ep", "dp", None),
    )
    out_specs = (P("ep", "dp", None), P(("ep", "dp"), None))
    return jax.shard_map(
        per_device, mesh=mesh, in_specs=in_specs, out_specs=out_specs, check_vma=False
    )
```

```python
import jax
import jax.numpy as jnp
from jax import lax
from jax.experimental import pallas as pl
from jax.experimental.pallas import tpu as pltpu
from jax.sharding import PartitionSpec as P

beta_one = 0.9
beta_two = 0.95
learn_rate = 0.2
decay_rate = 0.1
step_count = 100.0
adam_eps = 1e-08
zloss_coef = 0.25

LANE = 128
HALF = 64
META = 8
WIDE = 3
SPAN = WIDE * LANE
SCOPED = 56 << 20


def adamw(weight, first, second, gradient):
    first_new = beta_one * first.astype(jnp.float32) + (1.0 - beta_one) * gradient
    second_new = beta_two * second.astype(jnp.float32) + (1.0 - beta_two) * gradient * gradient
    first_hat = first_new * (1.0 / (1.0 - beta_one**step_count))
    second_hat = second_new * (1.0 / (1.0 - beta_two**step_count))
    current = weight.astype(jnp.float32)
    change = first_hat / (jnp.sqrt(second_hat) + adam_eps) + decay_rate * current
    return (current - learn_rate * change).astype(jnp.bfloat16)


def zloss_grad(logits):
    values = logits.astype(jnp.float32)
    row_max = jnp.max(values, axis=-1, keepdims=True)
    log_total = row_max + jnp.log(jnp.sum(jnp.exp(values - row_max), axis=-1, keepdims=True))
    probs = jnp.exp(values - log_total)
    return (zloss_coef * 2.0 * log_total * probs).astype(jnp.bfloat16)


def iota(shape, dim):
    return lax.broadcasted_iota(jnp.int32, shape, dim)


def digits(value, *bases):
    found = []
    for base in reversed(bases):
        above = jnp.floor((value.astype(jnp.float32) + 0.5) * (1.0 / base)).astype(jnp.int32)
        found.append(value - above * base)
        value = above
    return found[::-1]


def slots_of(ids):
    tokens = ids[0].shape[1]
    wide = [jnp.broadcast_to(row, (tokens, tokens)) for row in ids]
    tall = [jnp.transpose(mat) for mat in wide]
    earlier = iota((tokens, tokens), 0) < iota((tokens, tokens), 1)
    counts = []
    for mat in wide:
        hits = jnp.where(earlier & (tall[0] == mat), 1.0, 0.0)
        hits = hits + jnp.where(earlier & (tall[1] == mat), 1.0, 0.0)
        counts.append(jnp.sum(hits, axis=0, keepdims=True))
    return counts


def own_block(replicas):
    def body(ids_ref, combine_ref, grad_ref, message_ref):
        ids = ids_ref[...].astype(jnp.float32)
        combine = combine_ref[...]
        tokens = ids.shape[1]
        fold = tokens // 2
        pieces = [ids[0:1], ids[1:2]]
        for k in range(2):
            rest = combine[k : k + 1]
            for _ in range(3):
                part = rest.astype(jnp.bfloat16).astype(jnp.float32)
                pieces.append(part)
                rest = rest - part
        meta = jnp.concatenate(pieces, axis=0).astype(jnp.bfloat16)
        left = iota((fold, LANE), 1) < HALF
        size = WIDE * tokens + fold + META
        for j in range(replicas):
            base = j * size
            for t in range(WIDE):
                column = j * SPAN + t * LANE
                message_ref[base + t * tokens : base + (t + 1) * tokens, :] = grad_ref[
                    :, column : column + LANE
                ]
            column = replicas * SPAN + (j // 2) * LANE
            tile = grad_ref[:, column : column + LANE].astype(jnp.float32)
            turned = pltpu.roll(tile, HALF, 1)
            if j % 2 == 0:
                folded = jnp.where(left, tile[:fold], turned[fold:])
            else:
                folded = jnp.where(left, turned[:fold], tile[fold:])
            base += WIDE * tokens
            message_ref[base : base + fold, :] = folded.astype(jnp.bfloat16)
            message_ref[base + fold : base + fold + META, :] = meta

    return body


def own_columns(experts, capacity, replicas, tokens, group):
    part = replicas // 2
    height = part * capacity
    fold = tokens // 2

    def body(message_ref, send_ref, tokens_ref, target_ref, weight_ref):
        size = WIDE * tokens + fold + META
        for j in range(replicas):
            base, row = j * size, j * tokens
            for t in range(WIDE):
                tokens_ref[row : row + tokens, t * LANE : (t + 1) * LANE] = message_ref[
                    base + t * tokens : base + (t + 1) * tokens, :
                ]
            base += WIDE * tokens
            folded = message_ref[base : base + fold, :]
            turned = pltpu.roll(folded.astype(jnp.float32), HALF, 1).astype(jnp.bfloat16)
            tokens_ref[row : row + fold, SPAN : SPAN + LANE] = folded
            tokens_ref[row + fold : row + tokens, SPAN : SPAN + LANE] = turned
            meta = message_ref[base + fold : base + fold + META, 0:tokens].astype(jnp.float32)
            id_rows = [meta[0:1], meta[1:2]]
            slots = slots_of(id_rows)
            for k in range(2):
                where = id_rows[k] * height + slots[k] + float((j % part) * capacity)
                target_ref[k : k + 1, row : row + tokens] = where.astype(jnp.int32)
                first = 2 + 3 * k
                weight_ref[k : k + 1, row : row + tokens] = (
                    meta[first : first + 1] + meta[first + 1 : first + 2]
                ) + meta[first + 2 : first + 3]
        rows = group * height
        block = part * tokens
        total = 2 * WIDE * height + height
        left = iota((height, LANE), 1) < HALF

        def step(i, carry):
            key = iota((rows, block), 0) + i * rows
            lasts = []
            for h in range(2):
                columns = slice(h * block, (h + 1) * block)
                spread = jnp.where(
                    key == target_ref[0:1, columns],
                    weight_ref[0:1, columns],
                    jnp.where(key == target_ref[1:2, columns], weight_ref[1:2, columns], 0.0),
                )
                scale = jnp.sum(spread, axis=1, keepdims=True)
                chosen = jnp.where(spread > 0.0, 1.0, 0.0).astype(jnp.bfloat16)
                picked = jnp.dot(
                    chosen, tokens_ref[columns, :], preferred_element_type=jnp.float32
                )
                sent = picked * scale
                for g in range(group):
                    for t in range(WIDE):
                        start = (i * group + g) * total + (h * WIDE + t) * height
                        send_ref[pl.ds(pl.multiple_of(start, 8), height), :] = sent[
                            g * height : (g + 1) * height, t * LANE : (t + 1) * LANE
                        ].astype(jnp.bfloat16)
                lasts.append(sent[:, SPAN : SPAN + LANE])
            turned = pltpu.roll(lasts[1], HALF, 1)
            for g in range(group):
                place = slice(g * height, (g + 1) * height)
                start = (i * group + g) * total + 2 * WIDE * height
                send_ref[pl.ds(pl.multiple_of(start, 8), height), :] = jnp.where(
                    left, lasts[0][place], turned[place]
                ).astype(jnp.bfloat16)
            return carry

        lax.fori_loop(0, experts // group, step, 0, unroll=4 if experts // group % 4 == 0 else 1)

    return body


def split_state(replicas):
    def body(own_ref, *refs):
        inputs, outputs = refs[:3], list(refs[3:])
        part = replicas // 2
        size = outputs[0].shape[0]
        outputs += [outputs[part].at[pl.ds(r * size, size)] for r in range(1, part)]
        for a in range(3):
            rows = inputs[a].shape[0]
            height = WIDE * rows + rows // 2
            for r in range(replicas):
                owner = own_ref[0] ^ r
                for t in range(WIDE):
                    start = pl.multiple_of(owner * SPAN + t * LANE, LANE)
                    outputs[r][a * height + t * rows : a * height + (t + 1) * rows, :] = inputs[a][
                        :, pl.ds(start, LANE)
                    ]
                start = pl.multiple_of(replicas * SPAN + (owner >> 1) * LANE, LANE)
                tile = inputs[a][:, pl.ds(start, LANE)].astype(jnp.float32)
                turned = pltpu.roll(tile, HALF, 1)
                odd = jnp.broadcast_to(owner & 1, (rows // 2, LANE)) == 1
                low = jnp.where(odd, turned[: rows // 2], tile[: rows // 2])
                high = jnp.where(odd, tile[rows // 2 :], turned[rows // 2 :])
                left = iota((rows // 2, LANE), 1) < HALF
                outputs[r][a * height + WIDE * rows : (a + 1) * height, :] = jnp.where(
                    left, low, high
                ).astype(jnp.bfloat16)

    return body


def order_hidden(experts, capacity, replicas, group):
    rows = group * capacity
    part = replicas // 2
    total = part * rows
    runs = 2

    def body(own_ref, *refs):
        pieces, out_ref = refs[:replicas], refs[replicas]
        units = out_ref.shape[1]
        half, source, replica, slot = digits(iota((2 * total, 2 * total), 0), 2, group, part, capacity)
        origin = (half * part + replica) ^ own_ref[0]
        wanted = origin * rows + source * capacity + slot
        move = jnp.where(iota((2 * total, 2 * total), 1) == wanted, 1.0, 0.0)
        move = move.astype(jnp.bfloat16)
        steps = experts // group
        for i in range(steps):
            stacked = jnp.concatenate(
                [ref[i * rows : (i + 1) * rows, :] for ref in pieces], axis=0
            )
            moved = jnp.dot(move, stacked, preferred_element_type=jnp.float32)
            moved = jnp.transpose(moved).astype(jnp.bfloat16)
            run, place = i // (steps // runs), i % (steps // runs)
            for h in range(2):
                out_ref[2 * run + h, :, place * total : (place + 1) * total] = moved[
                    :, h * total : (h + 1) * total
                ]

    return body


def finish(experts, capacity, replicas, far):
    part = replicas // 2
    height = part * capacity
    runs = 2

    def body(own_ref, wide_ref, hidden_ref, *refs):
        state_hbm, next_hbm = refs[:replicas], refs[replicas : 2 * replicas]
        out_ref, units_ref, state_ref, next_ref, gradient_ref, updated_ref, sems = refs[
            2 * replicas :
        ]
        total = wide_ref.shape[0] // experts
        run_rows = experts // runs * total
        state_rows = state_hbm[0].shape[0]
        rows = next_hbm[0].shape[0] - far
        count = experts // runs * height
        copies = [
            pltpu.make_async_copy(hidden_ref.at[i], units_ref.at[i], sems.at[i])
            for i in range(2 * runs)
        ]
        for r in range(replicas):
            place = pl.ds(r * state_rows, state_rows)
            copies.append(
                pltpu.make_async_copy(
                    state_hbm[r], state_ref.at[place], sems.at[2 * runs + r]
                )
            )
        for r in range(replicas):
            copies.append(
                pltpu.make_async_copy(
                    next_hbm[r].at[pl.ds(far, rows)],
                    next_ref.at[pl.ds(r * rows, rows)],
                    sems.at[2 * runs + replicas + r],
                )
            )
        for copy in copies:
            copy.start()
        blocks = []
        for run in range(runs):
            received = wide_ref[run * run_rows : (run + 1) * run_rows, :]
            received = received.reshape(experts // runs, total, LANE)
            last = received[:, 2 * WIDE * height : total, :].reshape(count, LANE)
            for h in range(2):
                tiles = [
                    received[:, (h * WIDE + t) * height : (h * WIDE + t + 1) * height, :].reshape(
                        count, LANE
                    )
                    for t in range(WIDE)
                ]
                blocks.append(jnp.concatenate(tiles + [last], axis=1))
        slab = state_rows * 2 // (3 * (2 * WIDE + 1))
        piece = WIDE * slab + slab // 2
        per = replicas // 2
        for m in range(2):
            units = slice(m * per * slab, (m + 1) * per * slab)
            for i, block in enumerate(blocks):
                if m == 0:
                    copies[i].wait()
                product = jnp.dot(
                    units_ref[i, units, :], block, preferred_element_type=jnp.float32
                )
                if i % 2 == 1:
                    turned = pltpu.roll(product[:, SPAN : SPAN + LANE], HALF, 1)
                    product = jnp.concatenate([product[:, :SPAN], turned], axis=1)
                if i == 0:
                    gradient_ref[units, :] = product
                else:
                    gradient_ref[units, :] += product
            if m == 0:
                for copy in copies[2 * runs : 2 * runs + replicas]:
                    copy.wait()
            for s in range(m * per, (m + 1) * per):
                first = (own_ref[0] ^ s) * state_rows
                place = slice(s * slab, (s + 1) * slab)
                for t in range(WIDE + 1):
                    state = []
                    for a in range(3):
                        base = pl.multiple_of(first + a * piece + t * slab, 16)
                        if t < WIDE:
                            state.append(state_ref[pl.ds(base, slab), :])
                        else:
                            folded = state_ref[pl.ds(base, slab // 2), :].astype(jnp.float32)
                            state.append(
                                jnp.concatenate([folded, pltpu.roll(folded, HALF, 1)], axis=0)
                            )
                    columns = slice(t * LANE, (t + 1) * LANE)
                    updated_ref[place, columns] = adamw(*state, gradient_ref[place, columns])
        for copy in copies[2 * runs + replicas :]:
            copy.wait()
        result = jnp.dot(next_ref[...], updated_ref[...], preferred_element_type=jnp.float32)
        for r in range(replicas):
            start = pl.multiple_of((own_ref[0] ^ r) * rows, 16)
            out_ref[pl.ds(start, rows), :] = result[r * rows : (r + 1) * rows, :].astype(
                jnp.bfloat16
            )

    return body


def join_columns(replicas):
    def body(pieces_ref, out_ref):
        rows = out_ref.shape[0]
        left = iota((rows, LANE), 1) < HALF
        for j in range(replicas):
            out_ref[:, j * SPAN : (j + 1) * SPAN] = pieces_ref[j * rows : (j + 1) * rows, 0:SPAN]
            if j % 2 == 0:
                low, high = [
                    pieces_ref[(j + s) * rows : (j + s + 1) * rows, SPAN : SPAN + LANE].astype(
                        jnp.float32
                    )
                    for s in (0, 1)
                ]
                start = replicas * SPAN + (j // 2) * LANE
                out_ref[:, start : start + LANE] = jnp.where(
                    left, low, pltpu.roll(high, HALF, 1)
                ).astype(jnp.bfloat16)

    return body


def per_device(
    out_grad,
    expert_ids,
    combine,
    router_logits,
    saved_hidden,
    weight,
    moment_one,
    moment_two,
    next_hidden,
    interpret=False,
):
    experts = lax.axis_size("ep")
    replicas = lax.axis_size("dp")
    rows_total = saved_hidden.shape[1]
    capacity = rows_total // experts
    tokens = out_grad.shape[0]
    slab_rows = weight.shape[1]
    ff_width = saved_hidden.shape[2]
    next_rows = next_hidden.shape[1]
    part = replicas // 2
    message_rows = WIDE * tokens + tokens // 2 + META
    expert_rows = (2 * WIDE + 1) * part * capacity
    state_rows = 3 * (WIDE * slab_rows + slab_rows // 2)
    vmem = pl.BlockSpec(memory_space=pltpu.VMEM)
    smem = pl.BlockSpec(memory_space=pltpu.SMEM)
    hbm = pl.BlockSpec(memory_space=pl.ANY)
    own = lax.axis_index("dp").astype(jnp.int32).reshape(1)

    def near(value):
        return value if interpret else pltpu.with_memory_space_constraint(value, pltpu.VMEM)

    def call(body, ins, outs, scratch=(), scalar=False, local=False, last=False, specs=None):
        kind = pltpu.VMEM if local and not interpret and not last else jax.ShapeDtypeStruct
        shapes = [kind(shape, dtype) for shape, dtype in outs]
        single = len(shapes) == 1
        specs = specs or [vmem] * len(ins)
        if scalar:
            specs, ins = [smem] + specs, [own] + list(ins)
        return pl.pallas_call(
            body,
            out_shape=shapes[0] if single else tuple(shapes),
            in_specs=specs,
            out_specs=vmem if single else (vmem,) * len(shapes),
            scratch_shapes=list(scratch),
            compiler_params=pltpu.CompilerParams(vmem_limit_bytes=SCOPED if local else None),
            interpret=interpret,
        )(*ins)

    def send(value, r):
        return lax.ppermute(value, "dp", [(i, i ^ r) for i in range(replicas)])

    def tie(*values):
        return lax.optimization_barrier(values)

    def spread(value, pieces, across):
        if part != 4:
            return [value, send(value, part)], [pieces[0], send(across, part)]
        first = (send(value, part), send(value, 1), send(value, 3))
        moved = {r: send(pieces[r], r) for r in (1, 3)}
        far0, near1, near3, moved[1], moved[3], across, last = tie(
            *first, moved[1], moved[3], across, pieces[2]
        )
        far1, far3, across = send(far0, 1), send(far0, 3), send(across, part)
        far1, far3, near3, last = tie(far1, far3, near3, last)
        far2, near2 = send(far1, 3), send(near3, 1)
        far2, near2, across, last = tie(far2, near2, across, last)
        across = [across[q * state_rows : (q + 1) * state_rows] for q in range(part)]
        moved.update({0: pieces[0], 2: send(last, 2), 4: across[0]})
        moved.update({part + q: send(across[q], q) for q in (1, 3, 2)})
        gathered = [value, near1, near2, near3, far0, far1, far2, far3]
        return gathered, [moved[r] for r in range(replicas)]

    def swap(value, axis):
        parts = lax.axis_size(axis)
        value = value.reshape(parts, value.shape[0] // parts, value.shape[1])
        value = lax.all_to_all(value, axis, split_axis=0, concat_axis=0, tiled=True)
        return value.reshape(-1, value.shape[2])

    half16 = jnp.bfloat16
    message = call(
        own_block(replicas),
        [expert_ids.T, combine.T, out_grad],
        [((replicas * message_rows, LANE), half16)],
        local=True,
    )
    message = swap(message, "dp")
    hidden = jnp.concatenate([saved_hidden[0], next_hidden[0]], axis=0)
    state = call(
        split_state(replicas),
        [weight[0], moment_one[0], moment_two[0]],
        [((state_rows, LANE), half16)] * part + [((part * state_rows, LANE), half16)],
        scalar=True,
    )
    message, hidden, *state = tie(message, hidden, *state)
    wide = call(
        own_columns(experts, capacity, replicas, tokens, 8),
        [near(message)],
        [((experts * expert_rows, LANE), half16)],
        [
            pltpu.VMEM((replicas * tokens, SPAN + LANE), half16),
            pltpu.VMEM((2, replicas * tokens), jnp.int32),
            pltpu.VMEM((2, replicas * tokens), jnp.float32),
        ],
        local=True,
    )
    wide = swap(wide, "ep")
    hidden, state = spread(hidden, state[:part], state[part])

    runs = 2
    ordered = call(
        order_hidden(experts, capacity, replicas, 8),
        hidden,
        [((2 * runs, ff_width, part * rows_total // runs), half16)],
        scalar=True,
    )
    result = call(
        finish(experts, capacity, replicas, rows_total),
        [near(wide), ordered] + state + hidden,
        [((replicas * next_rows, SPAN + LANE), half16)],
        [
            pltpu.VMEM((2 * runs, ff_width, part * rows_total // runs), half16),
            pltpu.VMEM((replicas * state_rows, LANE), half16),
            pltpu.VMEM((replicas * next_rows, ff_width), half16),
            pltpu.VMEM((ff_width, SPAN + LANE), jnp.float32),
            pltpu.VMEM((ff_width, SPAN + LANE), half16),
            pltpu.SemaphoreType.DMA((2 * runs + 2 * replicas,)),
        ],
        scalar=True,
        local=True,
        specs=[vmem] + [hbm] * (1 + 2 * replicas),
    )
    result = swap(result, "dp")
    refreshed = call(
        join_columns(replicas),
        [near(result)],
        [((next_rows, out_grad.shape[1]), half16)],
        local=True,
        last=True,
    )
    return (refreshed[None], zloss_grad(router_logits))


def solution(mesh):
    in_specs = (
        P(("ep", "dp"), None),
        P(("ep", "dp"), None),
        P(("ep", "dp"), None),
        P(("ep", "dp"), None),
        P("ep", "dp", None),
        P("ep", "dp", None),
        P("ep", "dp", None),
        P("ep", "dp", None),
        P("ep", "dp", None),
    )
    out_specs = (P("ep", "dp", None), P(("ep", "dp"), None))
    return jax.shard_map(
        per_device, mesh=mesh, in_specs=in_specs, out_specs=out_specs, check_vma=False
    )
```

```python
import jax
import jax.numpy as jnp
from jax import lax
from jax.experimental import pallas as pl
from jax.experimental.pallas import tpu as pltpu
from jax.sharding import PartitionSpec as P

beta_one = 0.9
beta_two = 0.95
learn_rate = 0.2
decay_rate = 0.1
step_count = 100.0
adam_eps = 1e-08
zloss_coef = 0.25

LANE = 128
HALF = 64
META = 8
WIDE = 3
SPAN = WIDE * LANE
SCOPED = 56 << 20


def adamw(weight, first, second, gradient):
    first_new = beta_one * first.astype(jnp.float32) + (1.0 - beta_one) * gradient
    second_new = beta_two * second.astype(jnp.float32) + (1.0 - beta_two) * gradient * gradient
    first_hat = first_new * (1.0 / (1.0 - beta_one**step_count))
    second_hat = second_new * (1.0 / (1.0 - beta_two**step_count))
    current = weight.astype(jnp.float32)
    change = first_hat / (jnp.sqrt(second_hat) + adam_eps) + decay_rate * current
    return (current - learn_rate * change).astype(jnp.bfloat16)


def zloss_grad(logits):
    values = logits.astype(jnp.float32)
    row_max = jnp.max(values, axis=-1, keepdims=True)
    log_total = row_max + jnp.log(jnp.sum(jnp.exp(values - row_max), axis=-1, keepdims=True))
    probs = jnp.exp(values - log_total)
    return (zloss_coef * 2.0 * log_total * probs).astype(jnp.bfloat16)


def iota(shape, dim):
    return lax.broadcasted_iota(jnp.int32, shape, dim)


def digits(value, *bases):
    found = []
    for base in reversed(bases):
        above = jnp.floor((value.astype(jnp.float32) + 0.5) * (1.0 / base)).astype(jnp.int32)
        found.append(value - above * base)
        value = above
    return found[::-1]


def slots_of(ids):
    tokens = ids[0].shape[1]
    wide = [jnp.broadcast_to(row, (tokens, tokens)) for row in ids]
    tall = [jnp.transpose(mat) for mat in wide]
    earlier = iota((tokens, tokens), 0) < iota((tokens, tokens), 1)
    counts = []
    for mat in wide:
        hits = jnp.where(earlier & (tall[0] == mat), 1.0, 0.0)
        hits = hits + jnp.where(earlier & (tall[1] == mat), 1.0, 0.0)
        counts.append(jnp.sum(hits, axis=0, keepdims=True))
    return counts


def own_block(replicas):
    def body(ids_ref, combine_ref, grad_ref, message_ref):
        ids = ids_ref[...].astype(jnp.float32)
        combine = combine_ref[...]
        tokens = ids.shape[1]
        fold = tokens // 2
        pieces = [ids[0:1], ids[1:2]]
        for k in range(2):
            rest = combine[k : k + 1]
            for _ in range(3):
                part = rest.astype(jnp.bfloat16).astype(jnp.float32)
                pieces.append(part)
                rest = rest - part
        meta = jnp.concatenate(pieces, axis=0).astype(jnp.bfloat16)
        left = iota((fold, LANE), 1) < HALF
        size = WIDE * tokens + fold + META
        for j in range(replicas):
            base = j * size
            for t in range(WIDE):
                column = j * SPAN + t * LANE
                message_ref[base + t * tokens : base + (t + 1) * tokens, :] = grad_ref[
                    :, column : column + LANE
                ]
            column = replicas * SPAN + (j // 2) * LANE
            tile = grad_ref[:, column : column + LANE].astype(jnp.float32)
            turned = pltpu.roll(tile, HALF, 1)
            if j % 2 == 0:
                folded = jnp.where(left, tile[:fold], turned[fold:])
            else:
                folded = jnp.where(left, turned[:fold], tile[fold:])
            base += WIDE * tokens
            message_ref[base : base + fold, :] = folded.astype(jnp.bfloat16)
            message_ref[base + fold : base + fold + META, :] = meta

    return body


def own_columns(experts, capacity, replicas, tokens, group):
    part = replicas // 2
    height = part * capacity
    fold = tokens // 2

    def body(message_ref, send_ref, tokens_ref, target_ref, weight_ref):
        size = WIDE * tokens + fold + META
        for j in range(replicas):
            base, row = j * size, j * tokens
            for t in range(WIDE):
                tokens_ref[row : row + tokens, t * LANE : (t + 1) * LANE] = message_ref[
                    base + t * tokens : base + (t + 1) * tokens, :
                ]
            base += WIDE * tokens
            folded = message_ref[base : base + fold, :]
            turned = pltpu.roll(folded.astype(jnp.float32), HALF, 1).astype(jnp.bfloat16)
            tokens_ref[row : row + fold, SPAN : SPAN + LANE] = folded
            tokens_ref[row + fold : row + tokens, SPAN : SPAN + LANE] = turned
            meta = message_ref[base + fold : base + fold + META, 0:tokens].astype(jnp.float32)
            id_rows = [meta[0:1], meta[1:2]]
            slots = slots_of(id_rows)
            for k in range(2):
                where = id_rows[k] * height + slots[k] + float((j % part) * capacity)
                target_ref[k : k + 1, row : row + tokens] = where.astype(jnp.int32)
                first = 2 + 3 * k
                weight_ref[k : k + 1, row : row + tokens] = (
                    meta[first : first + 1] + meta[first + 1 : first + 2]
                ) + meta[first + 2 : first + 3]
        rows = group * height
        block = part * tokens
        total = 2 * WIDE * height + height
        left = iota((height, LANE), 1) < HALF

        def step(i, carry):
            key = iota((rows, block), 0) + i * rows
            lasts = []
            for h in range(2):
                columns = slice(h * block, (h + 1) * block)
                spread = jnp.where(
                    key == target_ref[0:1, columns],
                    weight_ref[0:1, columns],
                    jnp.where(key == target_ref[1:2, columns], weight_ref[1:2, columns], 0.0),
                )
                scale = jnp.sum(spread, axis=1, keepdims=True)
                chosen = jnp.where(spread > 0.0, 1.0, 0.0).astype(jnp.bfloat16)
                picked = jnp.dot(
                    chosen, tokens_ref[columns, :], preferred_element_type=jnp.float32
                )
                sent = picked * scale
                for g in range(group):
                    for t in range(WIDE):
                        start = (i * group + g) * total + (h * WIDE + t) * height
                        send_ref[pl.ds(pl.multiple_of(start, 8), height), :] = sent[
                            g * height : (g + 1) * height, t * LANE : (t + 1) * LANE
                        ].astype(jnp.bfloat16)
                lasts.append(sent[:, SPAN : SPAN + LANE])
            turned = pltpu.roll(lasts[1], HALF, 1)
            for g in range(group):
                place = slice(g * height, (g + 1) * height)
                start = (i * group + g) * total + 2 * WIDE * height
                send_ref[pl.ds(pl.multiple_of(start, 8), height), :] = jnp.where(
                    left, lasts[0][place], turned[place]
                ).astype(jnp.bfloat16)
            return carry

        lax.fori_loop(0, experts // group, step, 0, unroll=True)

    return body


def split_state(replicas):
    def body(own_ref, *refs):
        inputs, outputs = refs[:3], list(refs[3:])
        part = replicas // 2
        size = outputs[0].shape[0]
        outputs += [outputs[part].at[pl.ds(r * size, size)] for r in range(1, part)]
        for a in range(3):
            rows = inputs[a].shape[0]
            height = WIDE * rows + rows // 2
            for r in range(replicas):
                owner = own_ref[0] ^ r
                for t in range(WIDE):
                    start = pl.multiple_of(owner * SPAN + t * LANE, LANE)
                    outputs[r][a * height + t * rows : a * height + (t + 1) * rows, :] = inputs[a][
                        :, pl.ds(start, LANE)
                    ]
                start = pl.multiple_of(replicas * SPAN + (owner >> 1) * LANE, LANE)
                tile = inputs[a][:, pl.ds(start, LANE)].astype(jnp.float32)
                turned = pltpu.roll(tile, HALF, 1)
                odd = jnp.broadcast_to(owner & 1, (rows // 2, LANE)) == 1
                low = jnp.where(odd, turned[: rows // 2], tile[: rows // 2])
                high = jnp.where(odd, tile[rows // 2 :], turned[rows // 2 :])
                left = iota((rows // 2, LANE), 1) < HALF
                outputs[r][a * height + WIDE * rows : (a + 1) * height, :] = jnp.where(
                    left, low, high
                ).astype(jnp.bfloat16)

    return body


def order_hidden(experts, capacity, replicas, group):
    rows = group * capacity
    part = replicas // 2
    total = part * rows
    runs = 2

    def body(own_ref, *refs):
        pieces, out_ref = refs[:replicas], refs[replicas]
        units = out_ref.shape[1]
        half, source, replica, slot = digits(iota((2 * total, 2 * total), 0), 2, group, part, capacity)
        origin = (half * part + replica) ^ own_ref[0]
        wanted = origin * rows + source * capacity + slot
        move = jnp.where(iota((2 * total, 2 * total), 1) == wanted, 1.0, 0.0)
        move = move.astype(jnp.bfloat16)
        steps = experts // group
        for i in range(steps):
            stacked = jnp.concatenate(
                [ref[i * rows : (i + 1) * rows, :] for ref in pieces], axis=0
            )
            moved = jnp.dot(move, stacked, preferred_element_type=jnp.float32)
            moved = jnp.transpose(moved).astype(jnp.bfloat16)
            run, place = i // (steps // runs), i % (steps // runs)
            for h in range(2):
                out_ref[2 * run + h, :, place * total : (place + 1) * total] = moved[
                    :, h * total : (h + 1) * total
                ]

    return body


def finish(experts, capacity, replicas, far):
    part = replicas // 2
    height = part * capacity
    runs = 2

    def body(own_ref, wide_ref, hidden_ref, *refs):
        state_hbm, next_hbm = refs[:replicas], refs[replicas : 2 * replicas]
        out_ref, units_ref, state_ref, next_ref, gradient_ref, updated_ref, sems = refs[
            2 * replicas :
        ]
        total = wide_ref.shape[0] // experts
        run_rows = experts // runs * total
        state_rows = state_hbm[0].shape[0]
        rows = next_hbm[0].shape[0] - far
        count = experts // runs * height
        copies = [
            pltpu.make_async_copy(hidden_ref.at[i], units_ref.at[i], sems.at[i])
            for i in range(2 * runs)
        ]
        for r in range(replicas):
            place = pl.ds(r * state_rows, state_rows)
            copies.append(
                pltpu.make_async_copy(
                    state_hbm[r], state_ref.at[place], sems.at[2 * runs + r]
                )
            )
        for r in range(replicas):
            copies.append(
                pltpu.make_async_copy(
                    next_hbm[r].at[pl.ds(far, rows)],
                    next_ref.at[pl.ds(r * rows, rows)],
                    sems.at[2 * runs + replicas + r],
                )
            )
        for copy in copies:
            copy.start()
        blocks = []
        for run in range(runs):
            received = wide_ref[run * run_rows : (run + 1) * run_rows, :]
            received = received.reshape(experts // runs, total, LANE)
            last = received[:, 2 * WIDE * height : total, :].reshape(count, LANE)
            for h in range(2):
                tiles = [
                    received[:, (h * WIDE + t) * height : (h * WIDE + t + 1) * height, :].reshape(
                        count, LANE
                    )
                    for t in range(WIDE)
                ]
                blocks.append(jnp.concatenate(tiles + [last], axis=1))
        slab = state_rows * 2 // (3 * (2 * WIDE + 1))
        piece = WIDE * slab + slab // 2
        per = replicas // 2
        for m in range(2):
            units = slice(m * per * slab, (m + 1) * per * slab)
            for i, block in enumerate(blocks):
                if m == 0:
                    copies[i].wait()
                product = jnp.dot(
                    units_ref[i, units, :], block, preferred_element_type=jnp.float32
                )
                if i % 2 == 1:
                    turned = pltpu.roll(product[:, SPAN : SPAN + LANE], HALF, 1)
                    product = jnp.concatenate([product[:, :SPAN], turned], axis=1)
                if i == 0:
                    gradient_ref[units, :] = product
                else:
                    gradient_ref[units, :] += product
            if m == 0:
                for copy in copies[2 * runs : 2 * runs + replicas]:
                    copy.wait()
            for s in range(m * per, (m + 1) * per):
                first = (own_ref[0] ^ s) * state_rows
                place = slice(s * slab, (s + 1) * slab)
                for t in range(WIDE + 1):
                    state = []
                    for a in range(3):
                        base = pl.multiple_of(first + a * piece + t * slab, 16)
                        if t < WIDE:
                            state.append(state_ref[pl.ds(base, slab), :])
                        else:
                            folded = state_ref[pl.ds(base, slab // 2), :].astype(jnp.float32)
                            state.append(
                                jnp.concatenate([folded, pltpu.roll(folded, HALF, 1)], axis=0)
                            )
                    columns = slice(t * LANE, (t + 1) * LANE)
                    updated_ref[place, columns] = adamw(*state, gradient_ref[place, columns])
        for copy in copies[2 * runs + replicas :]:
            copy.wait()
        result = jnp.dot(next_ref[...], updated_ref[...], preferred_element_type=jnp.float32)
        for r in range(replicas):
            start = pl.multiple_of((own_ref[0] ^ r) * rows, 16)
            out_ref[pl.ds(start, rows), :] = result[r * rows : (r + 1) * rows, :].astype(
                jnp.bfloat16
            )

    return body


def join_columns(replicas):
    def body(pieces_ref, out_ref):
        rows = out_ref.shape[0]
        left = iota((rows, LANE), 1) < HALF
        for j in range(replicas):
            out_ref[:, j * SPAN : (j + 1) * SPAN] = pieces_ref[j * rows : (j + 1) * rows, 0:SPAN]
            if j % 2 == 0:
                low, high = [
                    pieces_ref[(j + s) * rows : (j + s + 1) * rows, SPAN : SPAN + LANE].astype(
                        jnp.float32
                    )
                    for s in (0, 1)
                ]
                start = replicas * SPAN + (j // 2) * LANE
                out_ref[:, start : start + LANE] = jnp.where(
                    left, low, pltpu.roll(high, HALF, 1)
                ).astype(jnp.bfloat16)

    return body


def per_device(
    out_grad,
    expert_ids,
    combine,
    router_logits,
    saved_hidden,
    weight,
    moment_one,
    moment_two,
    next_hidden,
    interpret=False,
):
    experts = lax.axis_size("ep")
    replicas = lax.axis_size("dp")
    rows_total = saved_hidden.shape[1]
    capacity = rows_total // experts
    tokens = out_grad.shape[0]
    slab_rows = weight.shape[1]
    ff_width = saved_hidden.shape[2]
    next_rows = next_hidden.shape[1]
    part = replicas // 2
    message_rows = WIDE * tokens + tokens // 2 + META
    expert_rows = (2 * WIDE + 1) * part * capacity
    state_rows = 3 * (WIDE * slab_rows + slab_rows // 2)
    vmem = pl.BlockSpec(memory_space=pltpu.VMEM)
    smem = pl.BlockSpec(memory_space=pltpu.SMEM)
    hbm = pl.BlockSpec(memory_space=pl.ANY)
    own = lax.axis_index("dp").astype(jnp.int32).reshape(1)

    def near(value):
        return value if interpret else pltpu.with_memory_space_constraint(value, pltpu.VMEM)

    def call(body, ins, outs, scratch=(), scalar=False, local=False, last=False, specs=None):
        kind = pltpu.VMEM if local and not interpret and not last else jax.ShapeDtypeStruct
        shapes = [kind(shape, dtype) for shape, dtype in outs]
        single = len(shapes) == 1
        specs = specs or [vmem] * len(ins)
        if scalar:
            specs, ins = [smem] + specs, [own] + list(ins)
        return pl.pallas_call(
            body,
            out_shape=shapes[0] if single else tuple(shapes),
            in_specs=specs,
            out_specs=vmem if single else (vmem,) * len(shapes),
            scratch_shapes=list(scratch),
            compiler_params=pltpu.CompilerParams(vmem_limit_bytes=SCOPED if local else None),
            interpret=interpret,
        )(*ins)

    def send(value, r):
        return lax.ppermute(value, "dp", [(i, i ^ r) for i in range(replicas)])

    def tie(*values):
        return lax.optimization_barrier(values)

    def spread(value, pieces, across):
        if part != 4:
            return [value, send(value, part)], [pieces[0], send(across, part)]
        first = (send(value, part), send(value, 1), send(value, 3))
        moved = {r: send(pieces[r], r) for r in (1, 3)}
        far0, near1, near3, moved[1], moved[3], across, last = tie(
            *first, moved[1], moved[3], across, pieces[2]
        )
        far1, far3, across = send(far0, 1), send(far0, 3), send(across, part)
        far1, far3, near3, last = tie(far1, far3, near3, last)
        far2, near2 = send(far1, 3), send(near3, 1)
        far2, near2, across, last = tie(far2, near2, across, last)
        across = [across[q * state_rows : (q + 1) * state_rows] for q in range(part)]
        moved.update({0: pieces[0], 2: send(last, 2), 4: across[0]})
        moved.update({part + q: send(across[q], q) for q in (1, 3, 2)})
        gathered = [value, near1, near2, near3, far0, far1, far2, far3]
        return gathered, [moved[r] for r in range(replicas)]

    def swap(value, axis):
        parts = lax.axis_size(axis)
        value = value.reshape(parts, value.shape[0] // parts, value.shape[1])
        value = lax.all_to_all(value, axis, split_axis=0, concat_axis=0, tiled=True)
        return value.reshape(-1, value.shape[2])

    half16 = jnp.bfloat16
    message = call(
        own_block(replicas),
        [expert_ids.T, combine.T, out_grad],
        [((replicas * message_rows, LANE), half16)],
        local=True,
    )
    message = swap(message, "dp")
    hidden = jnp.concatenate([saved_hidden[0], next_hidden[0]], axis=0)
    state = call(
        split_state(replicas),
        [weight[0], moment_one[0], moment_two[0]],
        [((state_rows, LANE), half16)] * part + [((part * state_rows, LANE), half16)],
        scalar=True,
    )
    message, hidden, *state = tie(message, hidden, *state)
    wide = call(
        own_columns(experts, capacity, replicas, tokens, 8),
        [near(message)],
        [((experts * expert_rows, LANE), half16)],
        [
            pltpu.VMEM((replicas * tokens, SPAN + LANE), half16),
            pltpu.VMEM((2, replicas * tokens), jnp.int32),
            pltpu.VMEM((2, replicas * tokens), jnp.float32),
        ],
        local=True,
    )
    wide = swap(wide, "ep")
    hidden, state = spread(hidden, state[:part], state[part])

    runs = 2
    ordered = call(
        order_hidden(experts, capacity, replicas, 8),
        hidden,
        [((2 * runs, ff_width, part * rows_total // runs), half16)],
        scalar=True,
    )
    result = call(
        finish(experts, capacity, replicas, rows_total),
        [near(wide), ordered] + state + hidden,
        [((replicas * next_rows, SPAN + LANE), half16)],
        [
            pltpu.VMEM((2 * runs, ff_width, part * rows_total // runs), half16),
            pltpu.VMEM((replicas * state_rows, LANE), half16),
            pltpu.VMEM((replicas * next_rows, ff_width), half16),
            pltpu.VMEM((ff_width, SPAN + LANE), jnp.float32),
            pltpu.VMEM((ff_width, SPAN + LANE), half16),
            pltpu.SemaphoreType.DMA((2 * runs + 2 * replicas,)),
        ],
        scalar=True,
        local=True,
        specs=[vmem] + [hbm] * (1 + 2 * replicas),
    )
    result = swap(result, "dp")
    refreshed = call(
        join_columns(replicas),
        [near(result)],
        [((next_rows, out_grad.shape[1]), half16)],
        local=True,
        last=True,
    )
    return (refreshed[None], zloss_grad(router_logits))


def solution(mesh):
    in_specs = (
        P(("ep", "dp"), None),
        P(("ep", "dp"), None),
        P(("ep", "dp"), None),
        P(("ep", "dp"), None),
        P("ep", "dp", None),
        P("ep", "dp", None),
        P("ep", "dp", None),
        P("ep", "dp", None),
        P("ep", "dp", None),
    )
    out_specs = (P("ep", "dp", None), P(("ep", "dp"), None))
    return jax.shard_map(
        per_device, mesh=mesh, in_specs=in_specs, out_specs=out_specs, check_vma=False
    )
```
